32 devices in a mesh: gx: 4 (over z), gy: 4 (over y, x), gz: 2 (over core).
Axes of the slice: x: 2, y: 2, z: 4, core: 2. Of those that a mesh axis runs over, the one named last changes fastest.
Arguments:
- rock_ids: int32 [16, 512, 512], P('gz', 'gx', 'gy'), may hold values from 0 to 7
- log_perm: float32 [16, 512, 512], P('gz', 'gx', 'gy'), may hold values from -3 to 3
- rock_diagonal: float32 [8, 3], replicated, may hold values from 0.2 to 5
- rock_shear: float32 [8, 3], replicated, may hold values from -0.8 to 0.8
- rock_storage: float32 [8], replicated, may hold values from 0.05 to 0.5
- source: float32 [16, 512, 512], P('gz', 'gx', 'gy'), may hold values from -6 to 6
- pressure_start: float32 [16, 512, 512], P('gz', 'gx', 'gy'), may hold values from -6 to 6
Outputs:
- pressure: float32 [16, 512, 512], P('gz', 'gx', 'gy')
- residual: float32 [16, 512, 512], P('gz', 'gx', 'gy')
The draws below stay inside these ranges and needn't reach their ends.
All inputs are finite; a program needn't handle non-finite values.
Results may differ from the reference program's by a relative error of at most 0.0003.
Values sent between devices are 32-bit elements; how exact they have to be, the bound alone decides.
A program may use at most 128 MiB of HBM per device.

```python
import math
import jax
import jax.numpy as jnp
from jax import lax

CZ = 8
CX = 128
CY = 128
CLASSES = 8
ITERS = 2
SWEEPS = 2
NZ = 16
NX = 512
NY = 512
N_GX = 4
N_GY = 4
N_GZ = 2


def place_ends(result, key, smallest, largest):
    index_at = [jax.random.randint(jax.random.fold_in(key, axis), (), 0, length) for axis, length in enumerate(result.shape)]
    widest = result.shape.index(max(result.shape))
    next_to = index_at[:widest] + [(index_at[widest] + 1) % result.shape[widest]] + index_at[widest + 1:]
    return result.at[tuple(index_at)].set(smallest).at[tuple(next_to)].set(largest)


def block_scale(rng, shape, pieces, low, top_value):
    factor_of = 1.0
    for dim, shards_of in pieces:
        steps = jax.random.uniform(jax.random.fold_in(jax.random.fold_in(rng, 6), dim), (shards_of,), jnp.float32, low / len(pieces), top_value / len(pieces))
        factor_of = factor_of * jnp.repeat(jnp.exp(steps), shape[dim] // shards_of).reshape((-1,) + (1,) * (len(shape) - 1 - dim))
    return factor_of


def centred(stream_key, extent, width, most, shards=(), held_as=jnp.bfloat16):
    gain = block_scale(stream_key, extent, shards, -0.22, 0.18) if shards else 1.0
    array = jax.random.normal(stream_key, extent, jnp.float32) * width * gain
    return jnp.minimum(jnp.maximum(array, -most), most).astype(held_as)


def setup_inputs(seed: int = 0) -> dict:
    streams_of = jax.random.split(jax.random.key(seed), 8)
    rock_ids = place_ends(jax.random.randint(streams_of[0], (NZ, NX, NY), 0, CLASSES), jax.random.fold_in(streams_of[0], 1), 0, CLASSES - 1).astype(jnp.int32)
    log_perm = centred(streams_of[1], (NZ, NX, NY), 1.0, 3.0, ((0, 2), (1, 4), (2, 4)), jnp.float32)
    rock_diagonal = jnp.clip(jnp.exp(jax.random.uniform(streams_of[2], (CLASSES, 3), jnp.float32, math.log(0.2), math.log(5.0))), 0.2, 5.0)
    rock_shear = jnp.clip(jax.random.uniform(streams_of[3], (CLASSES, 3), jnp.float32, -0.8, 0.8), -0.8, 0.8)
    rock_storage = jnp.clip(jnp.exp(jax.random.uniform(streams_of[4], (CLASSES,), jnp.float32, math.log(0.05), math.log(0.5))), 0.05, 0.5)
    source = centred(streams_of[5], (NZ, NX, NY), 1.0, 6.0, ((0, 2), (1, 4), (2, 4)), jnp.float32)
    pressure_start = centred(streams_of[6], (NZ, NX, NY), 1.0, 6.0, ((0, 2), (1, 4), (2, 4)), jnp.float32)
    return dict(rock_ids=rock_ids, log_perm=log_perm, rock_diagonal=rock_diagonal, rock_shear=rock_shear, rock_storage=rock_storage, source=source, pressure_start=pressure_start)


ROBIN = 0.5

def build_offsets():
    found = []
    for axis in range(3):
        for sign in (1, -1):
            vector = [0, 0, 0]
            vector[axis] = sign
            found.append((tuple(vector), axis, 1))
    for first, second, comp in ((0, 1, 3), (0, 2, 4), (1, 2, 5)):
        for sign_a in (1, -1):
            for sign_b in (1, -1):
                vector = [0, 0, 0]
                vector[first] = sign_a
                vector[second] = sign_b
                found.append((tuple(vector), comp, sign_a * sign_b))
    return found

def class_tables(rock_diagonal, rock_shear):
    col_z = rock_diagonal[:, 0]
    col_x = rock_diagonal[:, 1]
    col_y = rock_diagonal[:, 2]
    cross = jnp.sqrt(jnp.stack([col_z * col_x, col_z * col_y, col_x * col_y], axis=1))
    return jnp.concatenate([rock_diagonal, rock_shear * cross], axis=1)

def tensor_parts(ids, log_perm, table):
    parts = jnp.zeros((6,) + ids.shape, jnp.float32)
    zero = jnp.zeros((), jnp.float32)
    for klass in range(table.shape[0]):
        hit = (ids == klass)[None]
        parts = parts + jnp.where(hit, table[klass][:, None, None, None], zero)
    return parts * jnp.exp(log_perm)[None]

def class_value(ids, values):
    found = jnp.zeros(ids.shape, jnp.float32)
    for klass in range(values.shape[0]):
        found = jnp.where(ids == klass, values[klass], found)
    return found

def shifted(padded, vector):
    depth = padded.shape[-3] - 2
    rows = padded.shape[-2] - 2
    cols = padded.shape[-1] - 2
    return padded[..., 1 + vector[0]:1 + vector[0] + depth, 1 + vector[1]:1 + vector[1] + rows, 1 + vector[2]:1 + vector[2] + cols]

def border_masks(shape):
    masks = []
    for vector, comp, sign in build_offsets():
        mask = jnp.zeros(shape, bool)
        for axis in range(3):
            count = shape[axis]
            dims = [1, 1, 1]
            dims[axis] = count
            index = jnp.arange(count, dtype=jnp.int32).reshape(dims)
            if vector[axis] == 1:
                mask = mask | (index == count - 1)
            elif vector[axis] == -1:
                mask = mask | (index == 0)
        masks.append(mask)
    return masks

def prepare(kpad, storage):
    center = kpad[:, 1:-1, 1:-1, 1:-1]
    coefs = []
    for vector, comp, sign in build_offsets():
        near = shifted(kpad[comp], vector)
        if comp < 3:
            coef = 2.0 * center[comp] * near / (center[comp] + near)
        else:
            coef = 0.125 * sign * (center[comp] + near)
        coefs.append(coef)
    masks = border_masks(storage.shape)
    diag = storage
    robin = jnp.zeros(storage.shape, jnp.float32)
    for coef, mask in zip(coefs, masks):
        size = jnp.abs(coef)
        diag = diag + size
        robin = robin + jnp.where(mask, size, jnp.zeros((), jnp.float32))
    return (coefs, diag, ROBIN * robin)

def block_solve(coefs, diag, robin, source, ppad):
    old = ppad[1:-1, 1:-1, 1:-1]
    solution = old
    for sweep in range(SWEEPS):
        full = ppad.at[1:-1, 1:-1, 1:-1].set(solution)
        total = source + robin * old
        for coef, (vector, comp, sign) in zip(coefs, build_offsets()):
            total = total + coef * shifted(full, vector)
        solution = total / (diag + robin)
    return solution

def block_residual(coefs, diag, source, ppad):
    applied = diag * ppad[1:-1, 1:-1, 1:-1]
    for coef, (vector, comp, sign) in zip(coefs, build_offsets()):
        applied = applied - coef * shifted(ppad, vector)
    return source - applied

def reference(rock_ids, log_perm, rock_diagonal, rock_shear, rock_storage, source, pressure_start):
    table = class_tables(rock_diagonal, rock_shear)
    ids_pad = jnp.pad(rock_ids, 1, constant_values=-1)
    perm_pad = jnp.pad(log_perm, 1)
    nblocks = N_GZ * N_GX * N_GY

    def corner(block):
        zero_z = block // (N_GX * N_GY) * CZ
        zero_x = block // N_GY % N_GX * CX
        zero_y = block % N_GY * CY
        return (zero_z.astype(jnp.int32), zero_x.astype(jnp.int32), zero_y.astype(jnp.int32))

    def sweep_all(current, final):
        ppad = jnp.pad(current, 1)

        def one(block):
            starts = corner(block)
            ids_block = lax.dynamic_slice(ids_pad, starts, (CZ + 2, CX + 2, CY + 2))
            perm_block = lax.dynamic_slice(perm_pad, starts, (CZ + 2, CX + 2, CY + 2))
            kpad = tensor_parts(ids_block, perm_block, table)
            storage = class_value(ids_block[1:-1, 1:-1, 1:-1], rock_storage)
            coefs, diag, robin = prepare(kpad, storage)
            src = lax.dynamic_slice(source, starts, (CZ, CX, CY))
            pblock = lax.dynamic_slice(ppad, starts, (CZ + 2, CX + 2, CY + 2))
            if final:
                return block_residual(coefs, diag, src, pblock)
            return block_solve(coefs, diag, robin, src, pblock)
        blocks = lax.map(one, jnp.arange(nblocks, dtype=jnp.int32))
        blocks = blocks.reshape(N_GZ, N_GX, N_GY, CZ, CX, CY).transpose(0, 3, 1, 4, 2, 5)
        return blocks.reshape(N_GZ * CZ, N_GX * CX, N_GY * CY)
    pressure = pressure_start
    for step in range(ITERS):
        pressure = sweep_all(pressure, False)
    residual = sweep_all(pressure, True)
    return (pressure, residual)
```

```python
import itertools

import jax
import jax.numpy as jnp
from jax import lax
from jax.experimental import pallas as pl
from jax.experimental.pallas import tpu as pltpu
from jax.sharding import PartitionSpec as P

ITERS = 2
SWEEPS = 2
ROBIN = 0.5
AXES = ("gz", "gx", "gy")
LANES = 128


def build_offsets():
    found = []
    for axis in range(3):
        for sign in (1, -1):
            vector = [0, 0, 0]
            vector[axis] = sign
            found.append((tuple(vector), axis, 1))
    for first, second, comp in ((0, 1, 3), (0, 2, 4), (1, 2, 5)):
        for sign_a in (1, -1):
            for sign_b in (1, -1):
                vector = [0, 0, 0]
                vector[first] = sign_a
                vector[second] = sign_b
                found.append((tuple(vector), comp, sign_a * sign_b))
    return found


OFFSETS = build_offsets()
DIRS = [vector for vector, comp, sign in OFFSETS]
SLOT = {vector: index for index, vector in enumerate(DIRS)}
X_DIRS = [d for d in DIRS if d[1] != 0]
Y_DIRS = [d for d in DIRS if d[1] == 0 and d[2] != 0]
Z_DIRS = [d for d in DIRS if d[1] == 0 and d[2] == 0]
X_SLOT = {d: i for i, d in enumerate(X_DIRS)}
Y_SLOT = {d: i for i, d in enumerate(Y_DIRS)}
Z_SLOT = {d: i for i, d in enumerate(Z_DIRS)}


def make_kernel(sizes, shape, classes):
    cz, cx, cy = shape
    tiles = cx // 8
    top = cx + 8
    last = cz - 1

    def kernel(
        ids_ref, lp_ref, dia_ref, she_ref, sto_ref, src_ref, p_ref,
        out_ref, res_ref,
        tab, ten, ten_h, ten_p, ten_m, stor,
        va, vap, vam, vb, vbp, vbm, vh,
        coef, diag, robin, inv, base, pack,
        zs1, xs1, ys1, zl1, xl1, yl1,
        zs2, xs2, ys2, zl2, xl2, yl2,
        zs3, xs3, ys3, zl3, xl3, yl3,
        send_sem, recv_sem,
    ):
        here = [lax.axis_index(a) for a in AXES]

        def exists(d):
            ok = None
            for axis in range(3):
                if d[axis] == 1:
                    term = here[axis] < sizes[axis] - 1
                elif d[axis] == -1:
                    term = here[axis] > 0
                else:
                    continue
                ok = term if ok is None else jnp.logical_and(ok, term)
            return ok

        def target(d):
            return {a: here[i] + d[i] for i, a in enumerate(AXES) if d[i] != 0}

        there = {d: exists(d) for d in DIRS}
        barrier = pltpu.get_barrier_semaphore()

        for ref in (zl1, xl1, yl1, zl2, xl2, yl2, zl3, xl3, yl3):
            ref[...] = jnp.zeros_like(ref)

        expected = jnp.int32(0)
        for d in DIRS:
            @pl.when(there[d])
            def _(d=d):
                pl.semaphore_signal(
                    barrier, inc=1, device_id=target(d),
                    device_id_type=pl.DeviceIdType.MESH,
                )
            expected = expected + there[d].astype(jnp.int32)

        stages = (
            (zs1, xs1, ys1, zl1, xl1, yl1),
            (zs2, xs2, ys2, zl2, xl2, yl2),
            (zs3, xs3, ys3, zl3, xl3, yl3),
        )

        lane = lax.broadcasted_iota(jnp.int32, (cx, LANES), 1)

        def pack_faces(stage, q, plane, row):
            zs, xs, ys = stages[stage][:3]
            for side, z in ((0, 0), (1, last)):
                zs[side, q] = plane(z)
            for side, x in ((0, 0), (1, cx - 1)):
                xs[side, q] = row(x)
            mixed = jnp.zeros((cx, LANES), jnp.float32)
            for z in range(cz):
                moved = pltpu.roll(plane(z), 2 * z + 1, 1)
                mixed = jnp.where((lane // 2) == z, moved, mixed)
            ys[q] = mixed.T[: 2 * cz]

        def copy_of(stage, d):
            zs, xs, ys, zl, xl, yl = stages[stage]
            if d[1] != 0:
                src, dst = xs.at[(d[1] + 1) // 2], xl.at[X_SLOT[d]]
            elif d[2] != 0:
                src, dst = ys, yl.at[Y_SLOT[d]]
            else:
                src, dst = zs.at[(d[0] + 1) // 2], zl.at[Z_SLOT[d]]
            return pltpu.make_async_remote_copy(
                src_ref=src, dst_ref=dst,
                send_sem=send_sem.at[stage, SLOT[d]],
                recv_sem=recv_sem.at[stage, SLOT[d]],
                device_id=target(d), device_id_type=pl.DeviceIdType.MESH,
            )

        def opposite(d):
            return tuple(-c for c in d)

        def start(stage):
            for d in DIRS:
                @pl.when(there[d])
                def _(d=d):
                    copy_of(stage, d).start()

        def arrive(stage):
            for d in DIRS:
                @pl.when(there[opposite(d)])
                def _(d=d):
                    copy_of(stage, d).wait_recv()

        def getters(stage, q):
            zl, xl, yl = stages[stage][3:]

            def get_z(sz):
                return zl[Z_SLOT[(-sz, 0, 0)], q]

            def get_x(sx, sz, sy):
                return xl[X_SLOT[(-sz, -sx, -sy)], q]

            def get_y(sy, sz):
                return yl[Y_SLOT[(-sz, 0, -sy)], q]

            return get_z, get_x, get_y

        lane8 = lax.broadcasted_iota(jnp.int32, (cz, LANES), 1)
        even = lax.broadcasted_iota(jnp.int32, (2 * cz, LANES), 0) % 2 == 0

        def fill_center(field, get, has_z, has_x):
            get_z, get_x, get_y = get
            if has_z:
                for sz, z in ((-1, 0), (1, cz + 1)):
                    field[z, 8:top, :] = get_z(sz)
            if has_x:
                for sx, row in ((-1, 7), (1, top)):
                    field[1 : cz + 1, row, :] = get_x(sx, 0, 0)
                    if has_z:
                        field[0, row, :] = get_x(sx, -1, 0)[last]
                        field[cz + 1, row, :] = get_x(sx, 1, 0)[0]

        def fill_side(hold, get, has_z, has_x):
            get_z, get_x, get_y = get
            if has_x:
                for sx, row in ((-1, 7), (1, top)):
                    hold[1 : cz + 1, row, :] = jnp.where(
                        lane8 >= LANES // 2, get_x(sx, 0, -1), get_x(sx, 0, 1)
                    )
            pack[0 : 2 * cz, :] = jnp.where(even, get_y(-1, 0), get_y(1, 0))
            if has_z:
                pack[2 * cz : 4 * cz, :] = jnp.where(even, get_y(-1, -1), get_y(1, -1))
                pack[4 * cz : 6 * cz, :] = jnp.where(even, get_y(-1, 1), get_y(1, 1))
            turned = pack[...].T
            for z in range(cz):
                hold[z + 1, 8:top, :] = pltpu.roll(turned, LANES - 1 - 2 * z, 1)
            if has_z:
                hold[0, 8:top, :] = pltpu.roll(turned, LANES - 1 - (4 * cz - 2), 1)
                hold[cz + 1, 8:top, :] = pltpu.roll(turned, LANES - 1 - 4 * cz, 1)

        def shift_pair(value, side):
            spot = lax.broadcasted_iota(jnp.int32, value.shape, value.ndim - 1)
            ahead = pltpu.roll(jnp.where(spot == 0, side, value), LANES - 1, value.ndim - 1)
            behind = pltpu.roll(jnp.where(spot == LANES - 1, side, value), 1, value.ndim - 1)
            return ahead, behind

        pack_faces(
            0, 0,
            lambda z: (ids_ref[z] + 1).astype(jnp.float32),
            lambda x: (ids_ref[:, x, :] + 1).astype(jnp.float32),
        )
        pack_faces(0, 1, lambda z: lp_ref[z], lambda x: lp_ref[:, x, :])
        pack_faces(0, 2, lambda z: p_ref[z], lambda x: p_ref[:, x, :])

        pl.semaphore_wait(barrier, expected)
        start(0)

        for c in range(classes):
            cols = [jnp.full((8, LANES), dia_ref[c, k], jnp.float32) for k in range(3)]
            for k in range(3):
                tab[k, c] = cols[k]
            for k, (a, b) in enumerate(((0, 1), (0, 2), (1, 2))):
                tab[3 + k, c] = she_ref[c, k] * jnp.sqrt(cols[a] * cols[b])
            tab[6, c] = jnp.full((8, LANES), sto_ref[c], jnp.float32)

        def rows_of(t):
            return pl.ds(pl.multiple_of(t * 8, 8), 8)

        def lookup(code, comps):
            found = [jnp.zeros(code.shape, jnp.float32) for _ in comps]
            for c in range(classes):
                hit = code == jnp.float32(c + 1)
                found = [
                    jnp.where(hit, jnp.broadcast_to(tab[k, c, 0:1, :], code.shape), f)
                    for k, f in zip(comps, found)
                ]
            return found

        def tensor_tile(t, carry):
            r = rows_of(t)
            out = rows_of(t + 1)
            code = (ids_ref[:, r, :] + 1).astype(jnp.float32)
            gain = jnp.exp(lp_ref[:, r, :])
            found = lookup(code, range(7))
            for k in range(6):
                ten[k, 1 : cz + 1, out, :] = found[k] * gain
            stor[:, r, :] = found[6]
            va[1 : cz + 1, out, :] = p_ref[:, r, :]
            return carry

        lax.fori_loop(0, tiles, tensor_tile, 0)

        arrive(0)

        gid = getters(0, 0)
        glp = getters(0, 1)

        def tensor_get(k):
            def of(which):
                def get(*args):
                    code = gid[which](*args)
                    return lookup(code, [k])[0] * jnp.exp(glp[which](*args))
                return get
            return of(0), of(1), of(2)

        fill_center(ten.at[0], tensor_get(0), True, False)
        fill_center(ten.at[1], tensor_get(1), False, True)
        fill_center(ten.at[3], tensor_get(3), True, True)
        fill_center(ten.at[4], tensor_get(4), True, False)
        fill_center(ten.at[5], tensor_get(5), False, True)
        fill_side(ten_h.at[0], tensor_get(2), False, False)
        fill_side(ten_h.at[1], tensor_get(4), True, False)
        fill_side(ten_h.at[2], tensor_get(5), False, True)

        def tensor_shift(t, carry):
            r = rows_of(t)
            for slot, k in ((0, 2), (1, 4), (2, 5)):
                ahead, behind = shift_pair(ten[k, :, r, :], ten_h[slot, :, r, :])
                ten_p[slot, :, r, :] = ahead
                ten_m[slot, :, r, :] = behind
            return carry

        lax.fori_loop(0, tiles + 2, tensor_shift, 0)

        def load_halo(stage, q):
            get = getters(stage, q)
            fill_center(va, get, True, True)
            fill_side(vh, get, True, True)

            def shift(t, carry):
                r = rows_of(t)
                value = va[:, r, :]
                ahead, behind = shift_pair(value, vh[:, r, :])
                vap[:, r, :] = ahead
                vam[:, r, :] = behind
                for ref, got in ((vb, value), (vbp, ahead), (vbm, behind)):
                    ref[0, r, :] = got[0]
                    ref[cz + 1, r, :] = got[cz + 1]
                return carry

            lax.fori_loop(0, tiles + 2, shift, 0)
            for source, dest in ((va, vb), (vap, vbp), (vam, vbm)):
                for lo in (0, top):
                    dest[:, lo : lo + 8, :] = source[:, lo : lo + 8, :]

        def near_of(refs, t):
            plain, plus, minus = refs
            by_y = {0: plain, 1: plus, -1: minus}
            cache = {}

            def near(vector):
                dz, dx, dy = vector
                if (dx, dy) not in cache:
                    ref = by_y[dy]
                    r = pl.ds(t * 8 + 8 + dx, 8) if dx else rows_of(t + 1)
                    if dx and dy:
                        cache[(dx, dy)] = ref[1 : cz + 1, r, :]
                    else:
                        cache[(dx, dy)] = ref[:, r, :]
                got = cache[(dx, dy)]
                if dx and dy:
                    return got
                return got[1 + dz : 1 + dz + cz]

            return near

        zi = lax.broadcasted_iota(jnp.int32, (cz, 8, LANES), 0)
        xi = lax.broadcasted_iota(jnp.int32, (cz, 8, LANES), 1)
        yi = lax.broadcasted_iota(jnp.int32, (cz, 8, LANES), 2)

        def coef_tile(t, carry):
            r = rows_of(t)
            mid = rows_of(t + 1)
            at = (zi, xi + t * 8, yi)
            total = stor[:, r, :]
            rim = jnp.zeros((cz, 8, LANES), jnp.float32)
            nears = {
                0: near_of((ten.at[0], None, None), t),
                1: near_of((ten.at[1], None, None), t),
                2: near_of((ten.at[2], ten_p.at[0], ten_m.at[0]), t),
                3: near_of((ten.at[3], None, None), t),
                4: near_of((ten.at[4], ten_p.at[1], ten_m.at[1]), t),
                5: near_of((ten.at[5], ten_p.at[2], ten_m.at[2]), t),
            }
            for e, (vector, comp, sign) in enumerate(OFFSETS):
                own = ten[comp, 1 : cz + 1, mid, :]
                near = nears[comp](vector)
                if comp < 3:
                    value = 2.0 * own * near / (own + near)
                else:
                    value = 0.125 * sign * (own + near)
                coef[e, :, r, :] = value
                size = jnp.abs(value)
                total = total + size
                out = None
                for axis in range(3):
                    if vector[axis] == 0:
                        continue
                    edge = shape[axis] - 1 if vector[axis] == 1 else 0
                    hit = at[axis] == edge
                    out = hit if out is None else jnp.logical_or(out, hit)
                rim = rim + jnp.where(out, size, jnp.float32(0))
            rim = ROBIN * rim
            diag[:, r, :] = total
            robin[:, r, :] = rim
            inv[:, r, :] = 1.0 / (total + rim)
            return carry

        lax.fori_loop(0, tiles, coef_tile, 0)

        def gather(refs, t, acc):
            near = near_of(refs, t)
            r = rows_of(t)
            for e, (vector, comp, sign) in enumerate(OFFSETS):
                acc = acc + coef[e, :, r, :] * near(vector)
            return acc

        a_refs = (va, vap, vam)
        b_refs = (vb, vbp, vbm)

        def first_sweep(t, carry):
            r = rows_of(t)
            mid = rows_of(t + 1)
            steady = src_ref[:, r, :] + robin[:, r, :] * va[1 : cz + 1, mid, :]
            base[:, r, :] = steady
            u = gather(a_refs, t, steady) * inv[:, r, :]
            vb[1 : cz + 1, mid, :] = u
            ahead, behind = shift_pair(u, vh[1 : cz + 1, mid, :])
            vbp[1 : cz + 1, mid, :] = ahead
            vbm[1 : cz + 1, mid, :] = behind
            return carry

        def last_sweep(t, carry):
            r = rows_of(t)
            mid = rows_of(t + 1)
            u = gather(b_refs, t, base[:, r, :]) * inv[:, r, :]
            va[1 : cz + 1, mid, :] = u
            return carry

        for step in range(ITERS):
            load_halo(step, 2 if step == 0 else 0)
            lax.fori_loop(0, tiles, first_sweep, 0)
            lax.fori_loop(0, tiles, last_sweep, 0)
            pack_faces(
                step + 1, 0,
                lambda z: va[z + 1, 8:top, :],
                lambda x: va[1 : cz + 1, 8 + x, :],
            )
            start(step + 1)
            if step == ITERS - 1:
                out_ref[...] = va[1 : cz + 1, 8:top, :]
            arrive(step + 1)
        load_halo(ITERS, 0)

        def residual_tile(t, carry):
            r = rows_of(t)
            mid = rows_of(t + 1)
            applied = src_ref[:, r, :] - diag[:, r, :] * va[1 : cz + 1, mid, :]
            res_ref[:, r, :] = gather(a_refs, t, applied)
            return carry

        lax.fori_loop(0, tiles, residual_tile, 0)

        for stage in range(ITERS + 1):
            for d in DIRS:
                @pl.when(there[d])
                def _(d=d, stage=stage):
                    copy_of(stage, d).wait_send()

    return kernel


def solution(mesh):
    sizes = tuple(mesh.shape[a] for a in AXES)

    def per_device(rock_ids, log_perm, rock_diagonal, rock_shear, rock_storage, source, pressure_start):
        shape = rock_ids.shape
        cz, cx, cy = shape
        classes = rock_storage.shape[0]
        f32 = jnp.float32
        padded = (cz + 2, cx + 16, cy)

        def exchange(nq):
            return [
                pltpu.VMEM((2, nq, cx, cy), f32),
                pltpu.VMEM((2, nq, cz, cy), f32),
                pltpu.VMEM((nq, 2 * cz, cx), f32),
                pltpu.VMEM((len(Z_DIRS), nq, cx, cy), f32),
                pltpu.VMEM((len(X_DIRS), nq, cz, cy), f32),
                pltpu.VMEM((len(Y_DIRS), nq, 2 * cz, cx), f32),
            ]

        vmem = pl.BlockSpec(memory_space=pltpu.VMEM)
        smem = pl.BlockSpec(memory_space=pltpu.SMEM)
        return pl.pallas_call(
            make_kernel(sizes, shape, classes),
            out_shape=(jax.ShapeDtypeStruct(shape, f32), jax.ShapeDtypeStruct(shape, f32)),
            in_specs=[vmem, vmem, smem, smem, smem, vmem, vmem],
            out_specs=(vmem, vmem),
            scratch_shapes=[
                pltpu.VMEM((7, classes, 8, cy), f32),
                pltpu.VMEM((6,) + padded, f32),
                pltpu.VMEM((3,) + padded, f32),
                pltpu.VMEM((3,) + padded, f32),
                pltpu.VMEM((3,) + padded, f32),
                pltpu.VMEM(shape, f32),
            ]
            + [pltpu.VMEM(padded, f32)] * 7
            + [pltpu.VMEM((len(OFFSETS),) + shape, f32)]
            + [pltpu.VMEM(shape, f32)] * 4
            + [pltpu.VMEM((cx, cy), f32)]
            + exchange(3)
            + exchange(1)
            + exchange(1)
            + [
                pltpu.SemaphoreType.DMA((ITERS + 1, len(DIRS))),
                pltpu.SemaphoreType.DMA((ITERS + 1, len(DIRS))),
            ],
            compiler_params=pltpu.CompilerParams(
                collective_id=0, has_side_effects=True, vmem_limit_bytes=60 * 1024 * 1024
            ),
            name="schwarz",
        )(rock_ids, log_perm, rock_diagonal, rock_shear, rock_storage, source, pressure_start)

    block = P("gz", "gx", "gy")
    return jax.shard_map(
        per_device,
        mesh=mesh,
        in_specs=(block, block, P(), P(), P(), block, block),
        out_specs=(block, block),
        check_vma=False,
    )
```

```python
import itertools

import jax
import jax.numpy as jnp
from jax import lax
from jax.experimental import pallas as pl
from jax.experimental.pallas import tpu as pltpu
from jax.sharding import PartitionSpec as P

ITERS = 2
SWEEPS = 2
ROBIN = 0.5
AXES = ("gz", "gx", "gy")
LANES = 128


def build_offsets():
    found = []
    for axis in range(3):
        for sign in (1, -1):
            vector = [0, 0, 0]
            vector[axis] = sign
            found.append((tuple(vector), axis, 1))
    for first, second, comp in ((0, 1, 3), (0, 2, 4), (1, 2, 5)):
        for sign_a in (1, -1):
            for sign_b in (1, -1):
                vector = [0, 0, 0]
                vector[first] = sign_a
                vector[second] = sign_b
                found.append((tuple(vector), comp, sign_a * sign_b))
    return found


OFFSETS = build_offsets()
DIRS = [vector for vector, comp, sign in OFFSETS]
SLOT = {vector: index for index, vector in enumerate(DIRS)}
X_DIRS = [d for d in DIRS if d[1] != 0]
Y_DIRS = [d for d in DIRS if d[1] == 0 and d[2] != 0]
Z_DIRS = [d for d in DIRS if d[1] == 0 and d[2] == 0]
X_SLOT = {d: i for i, d in enumerate(X_DIRS)}
Y_SLOT = {d: i for i, d in enumerate(Y_DIRS)}
Z_SLOT = {d: i for i, d in enumerate(Z_DIRS)}


def make_kernel(sizes, shape, classes):
    cz, cx, cy = shape
    tiles = cx // 8
    top = cx + 8
    last = cz - 1

    def kernel(
        ids_ref, lp_ref, dia_ref, she_ref, sto_ref, src_ref, p_ref,
        out_ref, res_ref,
        tab, ten, ten_p, ten_m,
        va, vap, vam, vb, vbp, vbm,
        coef, diag, robin, inv, base, part, pack, zpad,
        rcx, rcy, rcz,
        zs1, xs1, ys1, zl1, xl1, yl1,
        zs2, xs2, ys2, zl2, xl2, yl2,
        zs3, xs3, ys3, zl3, xl3, yl3,
        send_sem, recv_sem,
    ):
        here = [lax.axis_index(a) for a in AXES]

        def exists(d):
            ok = None
            for axis in range(3):
                if d[axis] == 1:
                    term = here[axis] < sizes[axis] - 1
                elif d[axis] == -1:
                    term = here[axis] > 0
                else:
                    continue
                ok = term if ok is None else jnp.logical_and(ok, term)
            return ok

        def target(d):
            return {a: here[i] + d[i] for i, a in enumerate(AXES) if d[i] != 0}

        there = {d: exists(d) for d in DIRS}
        barrier = pltpu.get_barrier_semaphore()

        for ref in (zl1, xl1, yl1, zl2, xl2, yl2, zl3, xl3, yl3):
            ref[...] = jnp.zeros_like(ref)

        expected = jnp.int32(0)
        for d in DIRS:
            @pl.when(there[d])
            def _(d=d):
                pl.semaphore_signal(
                    barrier, inc=1, device_id=target(d),
                    device_id_type=pl.DeviceIdType.MESH,
                )
            expected = expected + there[d].astype(jnp.int32)

        stages = (
            (zs1, xs1, ys1, zl1, xl1, yl1),
            (zs2, xs2, ys2, zl2, xl2, yl2),
            (zs3, xs3, ys3, zl3, xl3, yl3),
        )

        lane = lax.broadcasted_iota(jnp.int32, (cx, LANES), 1)

        def pack_faces(stage, q, plane, row):
            zs, xs, ys = stages[stage][:3]
            for side, z in ((0, 0), (1, last)):
                zs[side, q] = plane(z)
            for side, x in ((0, 0), (1, cx - 1)):
                xs[side, q] = row(x)
            mixed = jnp.zeros((cx, LANES), jnp.float32)
            for z in range(cz):
                moved = pltpu.roll(plane(z), 2 * z + 1, 1)
                mixed = jnp.where((lane // 2) == z, moved, mixed)
            ys[q] = mixed.T[: 2 * cz]

        def copy_of(stage, d):
            zs, xs, ys, zl, xl, yl = stages[stage]
            if d[1] != 0:
                src, dst = xs.at[(d[1] + 1) // 2], xl.at[X_SLOT[d]]
            elif d[2] != 0:
                src, dst = ys, yl.at[Y_SLOT[d]]
            else:
                src, dst = zs.at[(d[0] + 1) // 2], zl.at[Z_SLOT[d]]
            return pltpu.make_async_remote_copy(
                src_ref=src, dst_ref=dst,
                send_sem=send_sem.at[stage, SLOT[d]],
                recv_sem=recv_sem.at[stage, SLOT[d]],
                device_id=target(d), device_id_type=pl.DeviceIdType.MESH,
            )

        def opposite(d):
            return tuple(-c for c in d)

        def start(stage):
            for d in reversed(DIRS):
                @pl.when(there[d])
                def _(d=d):
                    copy_of(stage, d).start()

        def arrive(stage):
            for d in DIRS:
                @pl.when(there[opposite(d)])
                def _(d=d):
                    copy_of(stage, d).wait_recv()

        def getters(stage, q):
            zl, xl, yl = stages[stage][3:]

            def get_z(sz):
                return zl[Z_SLOT[(-sz, 0, 0)], q]

            def get_x(sx, sz, sy):
                return xl[X_SLOT[(-sz, -sx, -sy)], q]

            def get_y(sy, sz):
                return yl[Y_SLOT[(-sz, 0, -sy)], q]

            return get_z, get_x, get_y

        lane_x = lax.broadcasted_iota(jnp.int32, (cz, LANES), 1)
        sub_x = lax.broadcasted_iota(jnp.int32, (cz, LANES), 0)
        lane_y = lax.broadcasted_iota(jnp.int32, (2 * cz, LANES), 1)
        sub_y = lax.broadcasted_iota(jnp.int32, (2 * cz, LANES), 0)
        even = sub_y % 2 == 0
        zero = jnp.float32(0)

        def turn(value):
            axis = value.ndim - 1
            return pltpu.roll(value, LANES - 1, axis), pltpu.roll(value, 1, axis)

        def near_x(get, sx, kinds):
            get_x = get[1]
            plain = get_x(sx, 0, 0)
            out = [plain]
            if "z" in kinds:
                out.append(jnp.where(sub_x < last, pltpu.roll(plain, cz - 1, 0), zero))
                out.append(jnp.where(sub_x > 0, pltpu.roll(plain, 1, 0), zero))
            if "y" in kinds:
                side = jnp.where(lane_x >= LANES // 2, get_x(sx, 0, -1), get_x(sx, 0, 1))
                out.append(pltpu.roll(jnp.where(lane_x == 0, side, plain), LANES - 1, 1))
                out.append(pltpu.roll(jnp.where(lane_x == LANES - 1, side, plain), 1, 1))
            return out

        def near_y(get, kinds):
            get_y = get[2]
            plain = jnp.where(
                even,
                pltpu.roll(get_y(1, 0), 2 * cz - 1, 0),
                pltpu.roll(get_y(-1, 0), 1, 0),
            )
            out = [plain]
            if "z" in kinds:
                out.append(jnp.where(sub_y < 2 * last, pltpu.roll(plain, 2 * cz - 2, 0), zero))
                out.append(jnp.where(sub_y >= 2, pltpu.roll(plain, 2, 0), zero))
            if "x" in kinds:
                ahead, behind = turn(plain)
                out.append(jnp.where(lane_y < LANES - 1, ahead, zero))
                out.append(jnp.where(lane_y > 0, behind, zero))
            return out

        def pack_sides(get):
            get_y = get[2]
            pack[2 * cz : 4 * cz, :] = jnp.where(even, get_y(-1, -1), get_y(1, -1))
            pack[4 * cz : 6 * cz, :] = jnp.where(even, get_y(-1, 1), get_y(1, 1))

        def near_z(get, sz, kinds, turned):
            get_z, get_x, get_y = get
            plain = get_z(sz)
            out = [plain]
            row = last if sz == -1 else 0
            if "x" in kinds:
                zpad[8:top, :] = plain
                zpad[7:8, :] = get_x(-1, sz, 0)[row : row + 1]
                zpad[top : top + 1, :] = get_x(1, sz, 0)[row : row + 1]
                out.append(zpad[9 : top + 1, :])
                out.append(zpad[7 : top - 1, :])
            if "y" in kinds:
                first = 4 * cz - 2 if sz == -1 else 4 * cz
                side = pltpu.roll(turned, LANES - 1 - first, 1)
                out.append(pltpu.roll(jnp.where(lane == 0, side, plain), LANES - 1, 1))
                out.append(pltpu.roll(jnp.where(lane == LANES - 1, side, plain), 1, 1))
            return out

        def harmonic(own, near):
            return 2.0 * own * near / (own + near)

        ends = jnp.logical_or(lane == 0, lane == LANES - 1)

        def spread(dest, add, turned, of_x, of_z):
            for z in range(cz):
                got = jnp.where(ends, pltpu.roll(turned, LANES - 1 - 2 * z, 1), zero)
                if z == 0:
                    got = got + of_z(-1)
                if z == last:
                    got = got + of_z(1)
                if add:
                    dest[z] += got
                else:
                    dest[z] = got
            for sx, row in ((-1, 0), (1, cx - 1)):
                dest[:, row, :] += of_x(sx)

        pack_faces(
            0, 0,
            lambda z: (ids_ref[z] + 1).astype(jnp.float32),
            lambda x: (ids_ref[:, x, :] + 1).astype(jnp.float32),
        )
        pack_faces(0, 1, lambda z: lp_ref[z], lambda x: lp_ref[:, x, :])
        pack_faces(0, 2, lambda z: p_ref[z], lambda x: p_ref[:, x, :])

        for c in range(classes):
            cols = [jnp.full((8, LANES), dia_ref[k, c], jnp.float32) for k in range(3)]
            for k in range(3):
                tab[k, c] = cols[k]
            for k, (a, b) in enumerate(((0, 1), (0, 2), (1, 2))):
                tab[3 + k, c] = she_ref[k, c] * jnp.sqrt(cols[a] * cols[b])
            tab[6, c] = jnp.full((8, LANES), sto_ref[c], jnp.float32)

        pack[...] = jnp.zeros_like(pack)
        for ref in (va, vap, vam, vb, vbp, vbm):
            for z in (0, cz + 1):
                ref[z] = jnp.zeros_like(ref[z])
            for lo in (0, top):
                ref[:, lo : lo + 8, :] = jnp.zeros((cz + 2, 8, LANES), jnp.float32)

        def rows_of(t):
            return pl.ds(pl.multiple_of(t * 8, 8), 8)

        def lookup(code, comps):
            found = [jnp.zeros(code.shape, jnp.float32) for _ in comps]
            for c in range(classes):
                hit = code == jnp.float32(c + 1)
                found = [
                    jnp.where(hit, jnp.broadcast_to(tab[k, c, 0:1, :], code.shape), f)
                    for k, f in zip(comps, found)
                ]
            return found

        def tensor_tile(t, carry):
            r = rows_of(t)
            out = rows_of(t + 1)
            code = (ids_ref[:, r, :] + 1).astype(jnp.float32)
            gain = jnp.exp(lp_ref[:, r, :])
            found = lookup(code, range(7))
            for k in range(6):
                value = found[k] * gain
                ten[k, 1 : cz + 1, out, :] = value
                if k in (2, 4, 5):
                    slot = (2, 4, 5).index(k)
                    ahead, behind = turn(value)
                    ten_p[slot, 1 : cz + 1, out, :] = ahead
                    ten_m[slot, 1 : cz + 1, out, :] = behind
            diag[:, r, :] = found[6]
            value = p_ref[:, r, :]
            ahead, behind = turn(value)
            va[1 : cz + 1, out, :] = value
            vap[1 : cz + 1, out, :] = ahead
            vam[1 : cz + 1, out, :] = behind
            return carry

        lax.fori_loop(0, tiles, tensor_tile, 0)

        pl.semaphore_wait(barrier, expected)
        start(0)

        def near_of(refs, t):
            plain, plus, minus = refs
            by_y = {0: plain, 1: plus, -1: minus}
            cache = {}

            def near(vector):
                dz, dx, dy = vector
                if (dx, dy) not in cache:
                    ref = by_y[dy]
                    r = pl.ds(t * 8 + 8 + dx, 8) if dx else rows_of(t + 1)
                    if dx and dy:
                        cache[(dx, dy)] = ref[1 : cz + 1, r, :]
                    else:
                        cache[(dx, dy)] = ref[:, r, :]
                got = cache[(dx, dy)]
                if dx and dy:
                    return got
                return got[1 + dz : 1 + dz + cz]

            return near

        zi = lax.broadcasted_iota(jnp.int32, (cz, 8, LANES), 0)
        xi = lax.broadcasted_iota(jnp.int32, (cz, 8, LANES), 1)
        yi = lax.broadcasted_iota(jnp.int32, (cz, 8, LANES), 2)

        def coef_tile(t, carry):
            r = rows_of(t)
            mid = rows_of(t + 1)
            at = (zi, xi + t * 8, yi)
            total = diag[:, r, :]
            nears = {
                0: near_of((ten.at[0], None, None), t),
                1: near_of((ten.at[1], None, None), t),
                2: near_of((ten.at[2], ten_p.at[0], ten_m.at[0]), t),
                3: near_of((ten.at[3], None, None), t),
                4: near_of((ten.at[4], ten_p.at[1], ten_m.at[1]), t),
                5: near_of((ten.at[5], ten_p.at[2], ten_m.at[2]), t),
            }
            for e, (vector, comp, sign) in enumerate(OFFSETS):
                own = ten[comp, 1 : cz + 1, mid, :]
                near = nears[comp](vector)
                if comp < 3:
                    value = harmonic(own, near)
                else:
                    value = 0.125 * sign * (own + near)
                out = None
                for axis in range(3):
                    if vector[axis] == 0:
                        continue
                    edge = shape[axis] - 1 if vector[axis] == 1 else 0
                    hit = at[axis] == edge
                    out = hit if out is None else jnp.logical_or(out, hit)
                value = jnp.where(out, zero, value)
                coef[e, :, r, :] = value
                total = total + jnp.abs(value)
            diag[:, r, :] = total
            return carry

        lax.fori_loop(0, tiles, coef_tile, 0)

        def gather(refs, t, acc):
            near = near_of(refs, t)
            r = rows_of(t)
            for e, (vector, comp, sign) in enumerate(OFFSETS):
                acc = acc + coef[e, :, r, :] * near(vector)
            return acc

        a_refs = (va, vap, vam)
        b_refs = (vb, vbp, vbm)

        def inside_tile(t, carry):
            r = rows_of(t)
            part[:, r, :] = gather(a_refs, t, src_ref[:, r, :])
            return carry

        lax.fori_loop(0, tiles, inside_tile, 0)

        arrive(0)

        gid = getters(0, 0)
        glp = getters(0, 1)

        def tensor_get(k):
            def of(which):
                def get(*args):
                    code = gid[which](*args)
                    return lookup(code, [k])[0] * jnp.exp(glp[which](*args))
                return get
            return of(0), of(1), of(2)

        gets = {k: tensor_get(k) for k in range(6)}
        rim_x = {}
        for side, sx in ((0, -1), (1, 1)):
            row = 8 if sx == -1 else top - 1
            own = {k: ten[k, 1 : cz + 1, row, :] for k in (1, 3, 5)}
            values = [harmonic(own[1], near_x(gets[1], sx, "")[0])]
            near = near_x(gets[3], sx, "z")
            for dz, got, ok in ((1, near[1], sub_x < last), (-1, near[2], sub_x > 0)):
                values.append(jnp.where(ok, 0.125 * (dz * sx) * (own[3] + got), zero))
            near = near_x(gets[5], sx, "y")
            for dy, got in ((1, near[1]), (-1, near[2])):
                values.append(0.125 * (sx * dy) * (own[5] + got))
            size = None
            for j, value in enumerate(values):
                rcx[side, j] = value
                size = jnp.abs(value) if size is None else size + jnp.abs(value)
            rim_x[sx] = size

        code = ys1[0]
        gain = jnp.exp(ys1[1])
        own = {k: f * gain for k, f in zip((2, 4, 5), lookup(code, (2, 4, 5)))}
        sy = jnp.where(even, jnp.float32(0.125), jnp.float32(-0.125))
        values = [harmonic(own[2], near_y(gets[2], "")[0])]
        near = near_y(gets[4], "z")
        for dz, got, ok in ((1, near[1], sub_y < 2 * last), (-1, near[2], sub_y >= 2)):
            values.append(jnp.where(ok, dz * sy * (own[4] + got), zero))
        near = near_y(gets[5], "x")
        for dx, got, ok in ((1, near[1], lane_y < LANES - 1), (-1, near[2], lane_y > 0)):
            values.append(jnp.where(ok, dx * sy * (own[5] + got), zero))
        size = None
        for j, value in enumerate(values):
            rcy[j] = value
            size = jnp.abs(value) if size is None else size + jnp.abs(value)
        pack[0 : 2 * cz, :] = size
        pack_sides(gets[4])
        turned = pack[...].T
        rim_z = {}
        for side, sz in ((0, -1), (1, 1)):
            z = 1 if sz == -1 else cz
            own = {k: ten[k, z, 8:top, :] for k in (0, 3, 4)}
            values = [harmonic(own[0], near_z(gets[0], sz, "", None)[0])]
            near = near_z(gets[3], sz, "x", None)
            for dx, got in ((1, near[1]), (-1, near[2])):
                values.append(0.125 * (sz * dx) * (own[3] + got))
            near = near_z(gets[4], sz, "y", turned)
            for dy, got in ((1, near[1]), (-1, near[2])):
                values.append(0.125 * (sz * dy) * (own[4] + got))
            size = None
            for j, value in enumerate(values):
                rcz[side, j] = value
                size = jnp.abs(value) if size is None else size + jnp.abs(value)
            rim_z[sz] = size
        spread(robin, False, turned, lambda sx: rim_x[sx], lambda sz: rim_z[sz])

        def scale_tile(t, carry):
            r = rows_of(t)
            rim = robin[:, r, :]
            total = diag[:, r, :] + rim
            rim = ROBIN * rim
            diag[:, r, :] = total
            robin[:, r, :] = rim
            inv[:, r, :] = 1.0 / (total + rim)
            return carry

        lax.fori_loop(0, tiles, scale_tile, 0)

        def weigh(weights, values):
            out = None
            for j, value in enumerate(values):
                term = weights(j) * value
                out = term if out is None else out + term
            return out

        def spread_pressure(dest, add, stage, q):
            get = getters(stage, q)
            pack[0 : 2 * cz, :] = weigh(lambda j: rcy[j], near_y(get, "zx"))
            pack_sides(get)
            turned = pack[...].T
            spread(
                dest, add, turned,
                lambda sx: weigh(lambda j: rcx[(sx + 1) // 2, j], near_x(get, sx, "zy")),
                lambda sz: weigh(lambda j: rcz[(sz + 1) // 2, j], near_z(get, sz, "xy", turned)),
            )

        def first_tile(t, carry):
            r = rows_of(t)
            mid = rows_of(t + 1)
            fixed = base[:, r, :] + robin[:, r, :] * va[1 : cz + 1, mid, :]
            u = (fixed + part[:, r, :]) * inv[:, r, :]
            base[:, r, :] = fixed + src_ref[:, r, :]
            ahead, behind = turn(u)
            vb[1 : cz + 1, mid, :] = u
            vbp[1 : cz + 1, mid, :] = ahead
            vbm[1 : cz + 1, mid, :] = behind
            return carry

        def second_tile(t, carry):
            r = rows_of(t)
            mid = rows_of(t + 1)
            u = gather(b_refs, t, base[:, r, :]) * inv[:, r, :]
            ahead, behind = turn(u)
            va[1 : cz + 1, mid, :] = u
            vap[1 : cz + 1, mid, :] = ahead
            vam[1 : cz + 1, mid, :] = behind
            return carry

        def residual_tile(t, carry):
            r = rows_of(t)
            value = va[1 : cz + 1, rows_of(t + 1), :]
            out_ref[:, r, :] = value
            applied = src_ref[:, r, :] - diag[:, r, :] * value
            res_ref[:, r, :] = gather(a_refs, t, applied)
            return carry

        for step in range(ITERS):
            spread_pressure(base, False, step, 2 if step == 0 else 0)
            lax.fori_loop(0, tiles, first_tile, 0)
            lax.fori_loop(0, tiles, second_tile, 0)
            pack_faces(
                step + 1, 0,
                lambda z: va[z + 1, 8:top, :],
                lambda x: va[1 : cz + 1, 8 + x, :],
            )
            start(step + 1)
            if step == ITERS - 1:
                lax.fori_loop(0, tiles, residual_tile, 0)
            else:
                lax.fori_loop(0, tiles, inside_tile, 0)
            arrive(step + 1)
        spread_pressure(res_ref, True, ITERS, 0)

        for stage in range(ITERS + 1):
            for d in DIRS:
                @pl.when(there[d])
                def _(d=d, stage=stage):
                    copy_of(stage, d).wait_send()

    return kernel


def solution(mesh):
    sizes = tuple(mesh.shape[a] for a in AXES)

    def per_device(rock_ids, log_perm, rock_diagonal, rock_shear, rock_storage, source, pressure_start):
        shape = rock_ids.shape
        cz, cx, cy = shape
        classes = rock_storage.shape[0]
        f32 = jnp.float32
        padded = (cz + 2, cx + 16, cy)

        def exchange(nq):
            return [
                pltpu.VMEM((2, nq, cx, cy), f32),
                pltpu.VMEM((2, nq, cz, cy), f32),
                pltpu.VMEM((nq, 2 * cz, cx), f32),
                pltpu.VMEM((len(Z_DIRS), nq, cx, cy), f32),
                pltpu.VMEM((len(X_DIRS), nq, cz, cy), f32),
                pltpu.VMEM((len(Y_DIRS), nq, 2 * cz, cx), f32),
            ]

        vmem = pl.BlockSpec(memory_space=pltpu.VMEM)
        smem = pl.BlockSpec(memory_space=pltpu.SMEM)
        return pl.pallas_call(
            make_kernel(sizes, shape, classes),
            out_shape=(jax.ShapeDtypeStruct(shape, f32), jax.ShapeDtypeStruct(shape, f32)),
            in_specs=[vmem, vmem, smem, smem, smem, vmem, vmem],
            out_specs=(vmem, vmem),
            scratch_shapes=[
                pltpu.VMEM((7, classes, 8, cy), f32),
                pltpu.VMEM((6,) + padded, f32),
                pltpu.VMEM((3,) + padded, f32),
                pltpu.VMEM((3,) + padded, f32),
            ]
            + [pltpu.VMEM(padded, f32)] * 6
            + [pltpu.VMEM((len(OFFSETS),) + shape, f32)]
            + [pltpu.VMEM(shape, f32)] * 5
            + [
                pltpu.VMEM((cx, cy), f32),
                pltpu.VMEM((cx + 16, cy), f32),
                pltpu.VMEM((2, 5, cz, cy), f32),
                pltpu.VMEM((5, 2 * cz, cx), f32),
                pltpu.VMEM((2, 5, cx, cy), f32),
            ]
            + exchange(3)
            + exchange(1)
            + exchange(1)
            + [
                pltpu.SemaphoreType.DMA((ITERS + 1, len(DIRS))),
                pltpu.SemaphoreType.DMA((ITERS + 1, len(DIRS))),
            ],
            compiler_params=pltpu.CompilerParams(
                collective_id=0, has_side_effects=True, vmem_limit_bytes=40 * 1024 * 1024
            ),
            name="schwarz",
        )(rock_ids, log_perm, rock_diagonal.T, rock_shear.T, rock_storage, source, pressure_start)

    block = P("gz", "gx", "gy")
    return jax.shard_map(
        per_device,
        mesh=mesh,
        in_specs=(block, block, P(), P(), P(), block, block),
        out_specs=(block, block),
        check_vma=False,
    )
```

```python
import itertools

import jax
import jax.numpy as jnp
from jax import lax
from jax.experimental import pallas as pl
from jax.experimental.pallas import tpu as pltpu
from jax.sharding import PartitionSpec as P

ITERS = 2
SWEEPS = 2
ROBIN = 0.5
AXES = ("gz", "gx", "gy")
LANES = 128


def build_offsets():
    found = []
    for axis in range(3):
        for sign in (1, -1):
            vector = [0, 0, 0]
            vector[axis] = sign
            found.append((tuple(vector), axis, 1))
    for first, second, comp in ((0, 1, 3), (0, 2, 4), (1, 2, 5)):
        for sign_a in (1, -1):
            for sign_b in (1, -1):
                vector = [0, 0, 0]
                vector[first] = sign_a
                vector[second] = sign_b
                found.append((tuple(vector), comp, sign_a * sign_b))
    return found


OFFSETS = build_offsets()
DIRS = [vector for vector, comp, sign in OFFSETS]
SLOT = {vector: index for index, vector in enumerate(DIRS)}
X_DIRS = [d for d in DIRS if d[1] != 0]
Y_DIRS = [d for d in DIRS if d[1] == 0 and d[2] != 0]
Z_DIRS = [d for d in DIRS if d[1] == 0 and d[2] == 0]
X_SLOT = {d: i for i, d in enumerate(X_DIRS)}
Y_SLOT = {d: i for i, d in enumerate(Y_DIRS)}
Z_SLOT = {d: i for i, d in enumerate(Z_DIRS)}
X_FIRST = sorted(X_DIRS, key=lambda d: -abs(d[2]))
YZ_DIRS = Y_DIRS + Z_DIRS


def make_kernel(sizes, shape, classes):
    cz, cx, cy = shape
    tiles = cx // 8
    top = cx + 8
    last = cz - 1

    def kernel(
        ids_hbm, lp_hbm, dia_ref, she_ref, sto_ref, src_hbm, p_hbm,
        out_hbm, res_hbm,
        tab, ten, ten_p, ten_m,
        va, vap, vam, vb, vbp, vbm,
        coef, diag, robin, inv, base, part, pack, zpad,
        rcx, rcy, rcz,
        zs1, xs1, ys1, zl1, xl1, yl1,
        zs2, xs2, ys2, zl2, xl2, yl2,
        zs3, xs3, ys3, zl3, xl3, yl3,
        ids_ref, lp_ref, src_ref, p_ref, res_ref, load_sem,
        send_sem, recv_sem,
    ):
        loads = [
            pltpu.make_async_copy(a, b, load_sem.at[i])
            for i, (a, b) in enumerate(
                ((ids_hbm, ids_ref), (lp_hbm, lp_ref), (p_hbm, p_ref), (src_hbm, src_ref))
            )
        ]
        for load in loads:
            load.start()
        here = [lax.axis_index(a) for a in AXES]

        def exists(d):
            ok = None
            for axis in range(3):
                if d[axis] == 1:
                    term = here[axis] < sizes[axis] - 1
                elif d[axis] == -1:
                    term = here[axis] > 0
                else:
                    continue
                ok = term if ok is None else jnp.logical_and(ok, term)
            return ok

        def target(d):
            return {a: here[i] + d[i] for i, a in enumerate(AXES) if d[i] != 0}

        there = {d: exists(d) for d in DIRS}
        barrier = pltpu.get_barrier_semaphore()

        for ref in (zl1, xl1, yl1, zl2, xl2, yl2, zl3, xl3, yl3):
            ref[...] = jnp.zeros_like(ref)

        expected = jnp.int32(0)
        for d in DIRS:
            @pl.when(there[d])
            def _(d=d):
                pl.semaphore_signal(
                    barrier, inc=1, device_id=target(d),
                    device_id_type=pl.DeviceIdType.MESH,
                )
            expected = expected + there[d].astype(jnp.int32)

        stages = (
            (zs1, xs1, ys1, zl1, xl1, yl1),
            (zs2, xs2, ys2, zl2, xl2, yl2),
            (zs3, xs3, ys3, zl3, xl3, yl3),
        )

        lane = lax.broadcasted_iota(jnp.int32, (cx, LANES), 1)

        def pack_faces(stage, q, plane, row):
            zs, xs, ys = stages[stage][:3]
            for side, z in ((0, 0), (1, last)):
                zs[side, q] = plane(z)
            if row is not None:
                for side, x in ((0, 0), (1, cx - 1)):
                    xs[side, q] = row(x)
            mixed = jnp.zeros((cx, LANES), jnp.float32)
            for z in range(cz):
                moved = pltpu.roll(plane(z), 2 * z + 1, 1)
                mixed = jnp.where((lane // 2) == z, moved, mixed)
            ys[q] = mixed.T[: 2 * cz]

        def copy_of(stage, d):
            zs, xs, ys, zl, xl, yl = stages[stage]
            if d[1] != 0:
                src, dst = xs.at[(d[1] + 1) // 2], xl.at[X_SLOT[d]]
            elif d[2] != 0:
                src, dst = ys, yl.at[Y_SLOT[d]]
            else:
                src, dst = zs.at[(d[0] + 1) // 2], zl.at[Z_SLOT[d]]
            return pltpu.make_async_remote_copy(
                src_ref=src, dst_ref=dst,
                send_sem=send_sem.at[stage, SLOT[d]],
                recv_sem=recv_sem.at[stage, SLOT[d]],
                device_id=target(d), device_id_type=pl.DeviceIdType.MESH,
            )

        def opposite(d):
            return tuple(-c for c in d)

        def start(stage, dirs):
            for d in dirs:
                @pl.when(there[d])
                def _(d=d):
                    copy_of(stage, d).start()

        def arrive(stage):
            for d in DIRS:
                @pl.when(there[opposite(d)])
                def _(d=d):
                    copy_of(stage, d).wait_recv()

        def getters(stage, q):
            zl, xl, yl = stages[stage][3:]

            def get_z(sz):
                return zl[Z_SLOT[(-sz, 0, 0)], q]

            def get_x(sx, sz, sy):
                return xl[X_SLOT[(-sz, -sx, -sy)], q]

            def get_y(sy, sz):
                return yl[Y_SLOT[(-sz, 0, -sy)], q]

            return get_z, get_x, get_y

        lane_x = lax.broadcasted_iota(jnp.int32, (cz, LANES), 1)
        sub_x = lax.broadcasted_iota(jnp.int32, (cz, LANES), 0)
        lane_y = lax.broadcasted_iota(jnp.int32, (2 * cz, LANES), 1)
        sub_y = lax.broadcasted_iota(jnp.int32, (2 * cz, LANES), 0)
        even = sub_y % 2 == 0
        zero = jnp.float32(0)

        def turn(value):
            axis = value.ndim - 1
            return pltpu.roll(value, LANES - 1, axis), pltpu.roll(value, 1, axis)

        def near_x(get, sx, kinds):
            get_x = get[1]
            plain = get_x(sx, 0, 0)
            out = [plain]
            if "z" in kinds:
                out.append(jnp.where(sub_x < last, pltpu.roll(plain, cz - 1, 0), zero))
                out.append(jnp.where(sub_x > 0, pltpu.roll(plain, 1, 0), zero))
            if "y" in kinds:
                side = jnp.where(lane_x >= LANES // 2, get_x(sx, 0, -1), get_x(sx, 0, 1))
                out.append(pltpu.roll(jnp.where(lane_x == 0, side, plain), LANES - 1, 1))
                out.append(pltpu.roll(jnp.where(lane_x == LANES - 1, side, plain), 1, 1))
            return out

        def near_y(get, kinds):
            get_y = get[2]
            plain = jnp.where(
                even,
                pltpu.roll(get_y(1, 0), 2 * cz - 1, 0),
                pltpu.roll(get_y(-1, 0), 1, 0),
            )
            out = [plain]
            if "z" in kinds:
                out.append(jnp.where(sub_y < 2 * last, pltpu.roll(plain, 2 * cz - 2, 0), zero))
                out.append(jnp.where(sub_y >= 2, pltpu.roll(plain, 2, 0), zero))
            if "x" in kinds:
                ahead, behind = turn(plain)
                out.append(jnp.where(lane_y < LANES - 1, ahead, zero))
                out.append(jnp.where(lane_y > 0, behind, zero))
            return out

        def pack_sides(get):
            get_y = get[2]
            pack[2 * cz : 4 * cz, :] = jnp.where(even, get_y(-1, -1), get_y(1, -1))
            pack[4 * cz : 6 * cz, :] = jnp.where(even, get_y(-1, 1), get_y(1, 1))

        def near_z(get, sz, kinds, turned):
            get_z, get_x, get_y = get
            plain = get_z(sz)
            out = [plain]
            row = last if sz == -1 else 0
            if "x" in kinds:
                zpad[8:top, :] = plain
                zpad[7:8, :] = get_x(-1, sz, 0)[row : row + 1]
                zpad[top : top + 1, :] = get_x(1, sz, 0)[row : row + 1]
                out.append(zpad[9 : top + 1, :])
                out.append(zpad[7 : top - 1, :])
            if "y" in kinds:
                first = 4 * cz - 2 if sz == -1 else 4 * cz
                side = pltpu.roll(turned, LANES - 1 - first, 1)
                out.append(pltpu.roll(jnp.where(lane == 0, side, plain), LANES - 1, 1))
                out.append(pltpu.roll(jnp.where(lane == LANES - 1, side, plain), 1, 1))
            return out

        def harmonic(own, near):
            return 2.0 * own * near / (own + near)

        ends = jnp.logical_or(lane == 0, lane == LANES - 1)

        def spread(dest, add, turned, of_x, of_z):
            for z in range(cz):
                got = jnp.where(ends, pltpu.roll(turned, LANES - 1 - 2 * z, 1), zero)
                if z == 0:
                    got = got + of_z(-1)
                if z == last:
                    got = got + of_z(1)
                if add:
                    dest[z] += got
                else:
                    dest[z] = got
            for sx, row in ((-1, 0), (1, cx - 1)):
                dest[:, row, :] += of_x(sx)

        for load in loads[:3]:
            load.wait()

        pack_faces(
            0, 0,
            lambda z: (ids_ref[z] + 1).astype(jnp.float32),
            lambda x: (ids_ref[:, x, :] + 1).astype(jnp.float32),
        )
        pack_faces(0, 1, lambda z: lp_ref[z], lambda x: lp_ref[:, x, :])
        pack_faces(0, 2, lambda z: p_ref[z], lambda x: p_ref[:, x, :])

        for c in range(classes):
            cols = [jnp.full((8, LANES), dia_ref[k, c], jnp.float32) for k in range(3)]
            for k in range(3):
                tab[k, c] = cols[k]
            for k, (a, b) in enumerate(((0, 1), (0, 2), (1, 2))):
                tab[3 + k, c] = she_ref[k, c] * jnp.sqrt(cols[a] * cols[b])
            tab[6, c] = jnp.full((8, LANES), sto_ref[c], jnp.float32)

        pack[...] = jnp.zeros_like(pack)
        for ref in (va, vap, vam, vb, vbp, vbm):
            for z in (0, cz + 1):
                ref[z] = jnp.zeros_like(ref[z])
            for lo in (0, top):
                ref[:, lo : lo + 8, :] = jnp.zeros((cz + 2, 8, LANES), jnp.float32)

        def rows_of(t):
            return pl.ds(pl.multiple_of(t * 8, 8), 8)

        def lookup(code, comps):
            found = [jnp.zeros(code.shape, jnp.float32) for _ in comps]
            for c in range(classes):
                hit = code == jnp.float32(c + 1)
                found = [
                    jnp.where(hit, jnp.broadcast_to(tab[k, c, 0:1, :], code.shape), f)
                    for k, f in zip(comps, found)
                ]
            return found

        def tensor_tile(t, carry):
            r = rows_of(t)
            out = rows_of(t + 1)
            code = (ids_ref[:, r, :] + 1).astype(jnp.float32)
            gain = jnp.exp(lp_ref[:, r, :])
            found = lookup(code, range(7))
            for k in range(6):
                value = found[k] * gain
                ten[k, 1 : cz + 1, out, :] = value
                if k in (2, 4, 5):
                    slot = (2, 4, 5).index(k)
                    ahead, behind = turn(value)
                    ten_p[slot, 1 : cz + 1, out, :] = ahead
                    ten_m[slot, 1 : cz + 1, out, :] = behind
            diag[:, r, :] = found[6]
            value = p_ref[:, r, :]
            ahead, behind = turn(value)
            va[1 : cz + 1, out, :] = value
            vap[1 : cz + 1, out, :] = ahead
            vam[1 : cz + 1, out, :] = behind
            return carry

        lax.fori_loop(0, tiles, tensor_tile, 0, unroll=2)

        pl.semaphore_wait(barrier, expected)
        start(0, X_FIRST + YZ_DIRS)

        def near_of(refs, t):
            plain, plus, minus = refs
            by_y = {0: plain, 1: plus, -1: minus}
            cache = {}

            def near(vector):
                dz, dx, dy = vector
                if (dx, dy) not in cache:
                    ref = by_y[dy]
                    r = pl.ds(t * 8 + 8 + dx, 8) if dx else rows_of(t + 1)
                    if dx and dy:
                        cache[(dx, dy)] = ref[1 : cz + 1, r, :]
                    else:
                        cache[(dx, dy)] = ref[:, r, :]
                got = cache[(dx, dy)]
                if dx and dy:
                    return got
                return got[1 + dz : 1 + dz + cz]

            return near

        zi = lax.broadcasted_iota(jnp.int32, (cz, 8, LANES), 0)
        xi = lax.broadcasted_iota(jnp.int32, (cz, 8, LANES), 1)
        yi = lax.broadcasted_iota(jnp.int32, (cz, 8, LANES), 2)

        def coef_tile(t, carry):
            r = rows_of(t)
            mid = rows_of(t + 1)
            at = (zi, xi + t * 8, yi)
            total = diag[:, r, :]
            nears = {
                0: near_of((ten.at[0], None, None), t),
                1: near_of((ten.at[1], None, None), t),
                2: near_of((ten.at[2], ten_p.at[0], ten_m.at[0]), t),
                3: near_of((ten.at[3], None, None), t),
                4: near_of((ten.at[4], ten_p.at[1], ten_m.at[1]), t),
                5: near_of((ten.at[5], ten_p.at[2], ten_m.at[2]), t),
            }
            for e, (vector, comp, sign) in enumerate(OFFSETS):
                own = ten[comp, 1 : cz + 1, mid, :]
                near = nears[comp](vector)
                if comp < 3:
                    value = harmonic(own, near)
                else:
                    value = 0.125 * sign * (own + near)
                out = None
                for axis in range(3):
                    if vector[axis] == 0:
                        continue
                    edge = shape[axis] - 1 if vector[axis] == 1 else 0
                    hit = at[axis] == edge
                    out = hit if out is None else jnp.logical_or(out, hit)
                value = jnp.where(out, zero, value)
                coef[e, :, r, :] = value
                total = total + jnp.abs(value)
            diag[:, r, :] = total
            return carry

        lax.fori_loop(0, tiles, coef_tile, 0)

        def gather(refs, t, acc):
            near = near_of(refs, t)
            r = rows_of(t)
            for e, (vector, comp, sign) in enumerate(OFFSETS):
                acc = acc + coef[e, :, r, :] * near(vector)
            return acc

        a_refs = (va, vap, vam)
        b_refs = (vb, vbp, vbm)

        loads[3].wait()

        def inside_tile(t, carry):
            r = rows_of(t)
            part[:, r, :] = gather(a_refs, t, src_ref[:, r, :])
            return carry

        lax.fori_loop(0, tiles, inside_tile, 0, unroll=2)

        arrive(0)

        gid = getters(0, 0)
        glp = getters(0, 1)

        def tensor_get(k):
            def of(which):
                def get(*args):
                    code = gid[which](*args)
                    return lookup(code, [k])[0] * jnp.exp(glp[which](*args))
                return get
            return of(0), of(1), of(2)

        gets = {k: tensor_get(k) for k in range(6)}
        rim_x = {}
        for side, sx in ((0, -1), (1, 1)):
            row = 8 if sx == -1 else top - 1
            own = {k: ten[k, 1 : cz + 1, row, :] for k in (1, 3, 5)}
            values = [harmonic(own[1], near_x(gets[1], sx, "")[0])]
            near = near_x(gets[3], sx, "z")
            for dz, got, ok in ((1, near[1], sub_x < last), (-1, near[2], sub_x > 0)):
                values.append(jnp.where(ok, 0.125 * (dz * sx) * (own[3] + got), zero))
            near = near_x(gets[5], sx, "y")
            for dy, got in ((1, near[1]), (-1, near[2])):
                values.append(0.125 * (sx * dy) * (own[5] + got))
            size = None
            for j, value in enumerate(values):
                rcx[side, j] = value
                size = jnp.abs(value) if size is None else size + jnp.abs(value)
            rim_x[sx] = size

        code = ys1[0]
        gain = jnp.exp(ys1[1])
        own = {k: f * gain for k, f in zip((2, 4, 5), lookup(code, (2, 4, 5)))}
        sy = jnp.where(even, jnp.float32(0.125), jnp.float32(-0.125))
        values = [harmonic(own[2], near_y(gets[2], "")[0])]
        near = near_y(gets[4], "z")
        for dz, got, ok in ((1, near[1], sub_y < 2 * last), (-1, near[2], sub_y >= 2)):
            values.append(jnp.where(ok, dz * sy * (own[4] + got), zero))
        near = near_y(gets[5], "x")
        for dx, got, ok in ((1, near[1], lane_y < LANES - 1), (-1, near[2], lane_y > 0)):
            values.append(jnp.where(ok, dx * sy * (own[5] + got), zero))
        size = None
        for j, value in enumerate(values):
            rcy[j] = value
            size = jnp.abs(value) if size is None else size + jnp.abs(value)
        pack[0 : 2 * cz, :] = size
        pack_sides(gets[4])
        turned = pack[...].T
        rim_z = {}
        for side, sz in ((0, -1), (1, 1)):
            z = 1 if sz == -1 else cz
            own = {k: ten[k, z, 8:top, :] for k in (0, 3, 4)}
            values = [harmonic(own[0], near_z(gets[0], sz, "", None)[0])]
            near = near_z(gets[3], sz, "x", None)
            for dx, got in ((1, near[1]), (-1, near[2])):
                values.append(0.125 * (sz * dx) * (own[3] + got))
            near = near_z(gets[4], sz, "y", turned)
            for dy, got in ((1, near[1]), (-1, near[2])):
                values.append(0.125 * (sz * dy) * (own[4] + got))
            size = None
            for j, value in enumerate(values):
                rcz[side, j] = value
                size = jnp.abs(value) if size is None else size + jnp.abs(value)
            rim_z[sz] = size
        spread(robin, False, turned, lambda sx: rim_x[sx], lambda sz: rim_z[sz])

        def scale_tile(t, carry):
            r = rows_of(t)
            rim = robin[:, r, :]
            total = diag[:, r, :] + rim
            rim = ROBIN * rim
            diag[:, r, :] = total
            robin[:, r, :] = rim
            inv[:, r, :] = 1.0 / (total + rim)
            return carry

        lax.fori_loop(0, tiles, scale_tile, 0, unroll=2)

        def weigh(weights, values):
            out = None
            for j, value in enumerate(values):
                term = weights(j) * value
                out = term if out is None else out + term
            return out

        def spread_pressure(dest, add, stage, q):
            get = getters(stage, q)
            pack[0 : 2 * cz, :] = weigh(lambda j: rcy[j], near_y(get, "zx"))
            pack_sides(get)
            turned = pack[...].T
            spread(
                dest, add, turned,
                lambda sx: weigh(lambda j: rcx[(sx + 1) // 2, j], near_x(get, sx, "zy")),
                lambda sz: weigh(lambda j: rcz[(sz + 1) // 2, j], near_z(get, sz, "xy", turned)),
            )

        def first_tile(t, carry):
            r = rows_of(t)
            mid = rows_of(t + 1)
            fixed = base[:, r, :] + robin[:, r, :] * va[1 : cz + 1, mid, :]
            u = (fixed + part[:, r, :]) * inv[:, r, :]
            base[:, r, :] = fixed + src_ref[:, r, :]
            ahead, behind = turn(u)
            vb[1 : cz + 1, mid, :] = u
            vbp[1 : cz + 1, mid, :] = ahead
            vbm[1 : cz + 1, mid, :] = behind
            return carry

        def second_tile(t, carry):
            r = rows_of(t)
            mid = rows_of(t + 1)
            u = gather(b_refs, t, base[:, r, :]) * inv[:, r, :]
            ahead, behind = turn(u)
            va[1 : cz + 1, mid, :] = u
            vap[1 : cz + 1, mid, :] = ahead
            vam[1 : cz + 1, mid, :] = behind
            return carry

        def residual_tile(t, carry):
            r = rows_of(t)
            value = va[1 : cz + 1, rows_of(t + 1), :]
            applied = src_ref[:, r, :] - diag[:, r, :] * value
            res_ref[:, r, :] = gather(a_refs, t, applied)
            return carry

        for step in range(ITERS):
            spread_pressure(base, False, step, 2 if step == 0 else 0)
            lax.fori_loop(0, tiles, first_tile, 0, unroll=2)
            lax.fori_loop(0, 2, lambda i, c: second_tile(i * (tiles - 1), c), 0, unroll=2)
            for side, x in ((0, 8), (1, top - 1)):
                stages[step + 1][1][side, 0] = va[1 : cz + 1, x, :]
            start(step + 1, X_FIRST)
            lax.fori_loop(1, tiles - 1, second_tile, 0, unroll=2)
            pack_faces(step + 1, 0, lambda z: va[z + 1, 8:top, :], None)
            start(step + 1, YZ_DIRS)
            if step == ITERS - 1:
                put_out = pltpu.make_async_copy(
                    va.at[1 : cz + 1, 8:top, :], out_hbm, load_sem.at[4]
                )
                put_out.start()
            if step == ITERS - 1:
                lax.fori_loop(0, tiles, residual_tile, 0, unroll=2)
            else:
                lax.fori_loop(0, tiles, inside_tile, 0, unroll=2)
            arrive(step + 1)
        spread_pressure(res_ref, True, ITERS, 0)
        put_res = pltpu.make_async_copy(res_ref, res_hbm, load_sem.at[5])
        put_res.start()
        put_out.wait()
        put_res.wait()

        for stage in range(ITERS + 1):
            for d in DIRS:
                @pl.when(there[d])
                def _(d=d, stage=stage):
                    copy_of(stage, d).wait_send()

    return kernel


def solution(mesh):
    sizes = tuple(mesh.shape[a] for a in AXES)

    def per_device(rock_ids, log_perm, rock_diagonal, rock_shear, rock_storage, source, pressure_start):
        shape = rock_ids.shape
        cz, cx, cy = shape
        classes = rock_storage.shape[0]
        f32 = jnp.float32
        padded = (cz + 2, cx + 16, cy)

        def exchange(nq):
            return [
                pltpu.VMEM((2, nq, cx, cy), f32),
                pltpu.VMEM((2, nq, cz, cy), f32),
                pltpu.VMEM((nq, 2 * cz, cx), f32),
                pltpu.VMEM((len(Z_DIRS), nq, cx, cy), f32),
                pltpu.VMEM((len(X_DIRS), nq, cz, cy), f32),
                pltpu.VMEM((len(Y_DIRS), nq, 2 * cz, cx), f32),
            ]

        hbm = pl.BlockSpec(memory_space=pltpu.HBM)
        smem = pl.BlockSpec(memory_space=pltpu.SMEM)
        return pl.pallas_call(
            make_kernel(sizes, shape, classes),
            out_shape=(jax.ShapeDtypeStruct(shape, f32), jax.ShapeDtypeStruct(shape, f32)),
            in_specs=[hbm, hbm, smem, smem, smem, hbm, hbm],
            out_specs=(hbm, hbm),
            scratch_shapes=[
                pltpu.VMEM((7, classes, 8, cy), f32),
                pltpu.VMEM((6,) + padded, f32),
                pltpu.VMEM((3,) + padded, f32),
                pltpu.VMEM((3,) + padded, f32),
            ]
            + [pltpu.VMEM(padded, f32)] * 6
            + [pltpu.VMEM((len(OFFSETS),) + shape, f32)]
            + [pltpu.VMEM(shape, f32)] * 5
            + [
                pltpu.VMEM((cx, cy), f32),
                pltpu.VMEM((cx + 16, cy), f32),
                pltpu.VMEM((2, 5, cz, cy), f32),
                pltpu.VMEM((5, 2 * cz, cx), f32),
                pltpu.VMEM((2, 5, cx, cy), f32),
            ]
            + exchange(3)
            + exchange(1)
            + exchange(1)
            + [pltpu.VMEM(shape, jnp.int32)]
            + [pltpu.VMEM(shape, f32)] * 4
            + [
                pltpu.SemaphoreType.DMA((6,)),
                pltpu.SemaphoreType.DMA((ITERS + 1, len(DIRS))),
                pltpu.SemaphoreType.DMA((ITERS + 1, len(DIRS))),
            ],
            compiler_params=pltpu.CompilerParams(
                collective_id=0, has_side_effects=True, vmem_limit_bytes=61440 * 1024
            ),
            name="schwarz",
        )(rock_ids, log_perm, rock_diagonal.T, rock_shear.T, rock_storage, source, pressure_start)

    block = P("gz", "gx", "gy")
    return jax.shard_map(
        per_device,
        mesh=mesh,
        in_specs=(block, block, P(), P(), P(), block, block),
        out_specs=(block, block),
        check_vma=False,
    )
```

```python
import itertools

import jax
import jax.numpy as jnp
from jax import lax
from jax.experimental import pallas as pl
from jax.experimental.pallas import tpu as pltpu
from jax.sharding import PartitionSpec as P

ITERS = 2
SWEEPS = 2
ROBIN = 0.5
AXES = ("gz", "gx", "gy")
LANES = 128


def build_offsets():
    found = []
    for axis in range(3):
        for sign in (1, -1):
            vector = [0, 0, 0]
            vector[axis] = sign
            found.append((tuple(vector), axis, 1))
    for first, second, comp in ((0, 1, 3), (0, 2, 4), (1, 2, 5)):
        for sign_a in (1, -1):
            for sign_b in (1, -1):
                vector = [0, 0, 0]
                vector[first] = sign_a
                vector[second] = sign_b
                found.append((tuple(vector), comp, sign_a * sign_b))
    return found


OFFSETS = build_offsets()
DIRS = [vector for vector, comp, sign in OFFSETS]
SLOT = {vector: index for index, vector in enumerate(DIRS)}
X_DIRS = [d for d in DIRS if d[1] != 0]
Y_DIRS = [d for d in DIRS if d[1] == 0 and d[2] != 0]
Z_DIRS = [d for d in DIRS if d[1] == 0 and d[2] == 0]
X_SLOT = {d: i for i, d in enumerate(X_DIRS)}
Y_SLOT = {d: i for i, d in enumerate(Y_DIRS)}
Z_SLOT = {d: i for i, d in enumerate(Z_DIRS)}
X_FIRST = sorted(X_DIRS, key=lambda d: -abs(d[2]))
YZ_DIRS = Y_DIRS + Z_DIRS


def make_kernel(sizes, shape, classes):
    cz, cx, cy = shape
    tiles = cx // 8
    top = cx + 8
    last = cz - 1

    def kernel(
        ids_hbm, lp_hbm, dia_ref, she_ref, sto_ref, src_hbm, p_hbm,
        out_hbm, res_hbm,
        tab, ten, ten_p, ten_m,
        va, vap, vam, vb, vbp, vbm,
        coef, diag, robin, inv, base, part, pack, zpad,
        rcx, rcy, rcz,
        zs1, xs1, ys1, zl1, xl1, yl1,
        zs2, xs2, ys2, zl2, xl2, yl2,
        zs3, xs3, ys3, zl3, xl3, yl3,
        ids_ref, lp_ref, src_ref, p_ref, res_ref, load_sem,
        send_sem, recv_sem,
    ):
        loads = [
            pltpu.make_async_copy(a, b, load_sem.at[i])
            for i, (a, b) in enumerate(
                ((ids_hbm, ids_ref), (lp_hbm, lp_ref), (p_hbm, p_ref), (src_hbm, src_ref))
            )
        ]
        for load in loads:
            load.start()
        here = [lax.axis_index(a) for a in AXES]

        def exists(d):
            ok = None
            for axis in range(3):
                if d[axis] == 1:
                    term = here[axis] < sizes[axis] - 1
                elif d[axis] == -1:
                    term = here[axis] > 0
                else:
                    continue
                ok = term if ok is None else jnp.logical_and(ok, term)
            return ok

        def target(d):
            return {a: here[i] + d[i] for i, a in enumerate(AXES) if d[i] != 0}

        there = {d: exists(d) for d in DIRS}
        barrier = pltpu.get_barrier_semaphore()

        for ref in (zl1, xl1, yl1, zl2, xl2, yl2, zl3, xl3, yl3):
            ref[...] = jnp.zeros_like(ref)

        expected = jnp.int32(0)
        for d in DIRS:
            @pl.when(there[d])
            def _(d=d):
                pl.semaphore_signal(
                    barrier, inc=1, device_id=target(d),
                    device_id_type=pl.DeviceIdType.MESH,
                )
            expected = expected + there[d].astype(jnp.int32)

        stages = (
            (zs1, xs1, ys1, zl1, xl1, yl1),
            (zs2, xs2, ys2, zl2, xl2, yl2),
            (zs3, xs3, ys3, zl3, xl3, yl3),
        )

        lane = lax.broadcasted_iota(jnp.int32, (cx, LANES), 1)

        def pack_faces(stage, q, plane, row):
            zs, xs, ys = stages[stage][:3]
            for side, z in ((0, 0), (1, last)):
                zs[side, q] = plane(z)
            if row is not None:
                for side, x in ((0, 0), (1, cx - 1)):
                    xs[side, q] = row(x)
            mixed = jnp.zeros((cx, LANES), jnp.float32)
            for z in range(cz):
                moved = pltpu.roll(plane(z), 2 * z + 1, 1)
                mixed = jnp.where((lane // 2) == z, moved, mixed)
            ys[q] = mixed.T[: 2 * cz]

        def copy_of(stage, d):
            zs, xs, ys, zl, xl, yl = stages[stage]
            if d[1] != 0:
                src, dst = xs.at[(d[1] + 1) // 2], xl.at[X_SLOT[d]]
            elif d[2] != 0:
                src, dst = ys, yl.at[Y_SLOT[d]]
            else:
                src, dst = zs.at[(d[0] + 1) // 2], zl.at[Z_SLOT[d]]
            return pltpu.make_async_remote_copy(
                src_ref=src, dst_ref=dst,
                send_sem=send_sem.at[stage, SLOT[d]],
                recv_sem=recv_sem.at[stage, SLOT[d]],
                device_id=target(d), device_id_type=pl.DeviceIdType.MESH,
            )

        def opposite(d):
            return tuple(-c for c in d)

        def start(stage, dirs):
            for d in dirs:
                @pl.when(there[d])
                def _(d=d):
                    copy_of(stage, d).start()

        def arrive(stage):
            for d in DIRS:
                @pl.when(there[opposite(d)])
                def _(d=d):
                    copy_of(stage, d).wait_recv()

        def getters(stage, q):
            zl, xl, yl = stages[stage][3:]

            def get_z(sz):
                return zl[Z_SLOT[(-sz, 0, 0)], q]

            def get_x(sx, sz, sy):
                return xl[X_SLOT[(-sz, -sx, -sy)], q]

            def get_y(sy, sz):
                return yl[Y_SLOT[(-sz, 0, -sy)], q]

            return get_z, get_x, get_y

        lane_x = lax.broadcasted_iota(jnp.int32, (cz, LANES), 1)
        sub_x = lax.broadcasted_iota(jnp.int32, (cz, LANES), 0)
        lane_y = lax.broadcasted_iota(jnp.int32, (2 * cz, LANES), 1)
        sub_y = lax.broadcasted_iota(jnp.int32, (2 * cz, LANES), 0)
        even = sub_y % 2 == 0
        zero = jnp.float32(0)

        def turn(value):
            axis = value.ndim - 1
            return pltpu.roll(value, LANES - 1, axis), pltpu.roll(value, 1, axis)

        def near_x(get, sx, kinds):
            get_x = get[1]
            plain = get_x(sx, 0, 0)
            out = [plain]
            if "z" in kinds:
                out.append(jnp.where(sub_x < last, pltpu.roll(plain, cz - 1, 0), zero))
                out.append(jnp.where(sub_x > 0, pltpu.roll(plain, 1, 0), zero))
            if "y" in kinds:
                side = jnp.where(lane_x >= LANES // 2, get_x(sx, 0, -1), get_x(sx, 0, 1))
                out.append(pltpu.roll(jnp.where(lane_x == 0, side, plain), LANES - 1, 1))
                out.append(pltpu.roll(jnp.where(lane_x == LANES - 1, side, plain), 1, 1))
            return out

        def near_y(get, kinds):
            get_y = get[2]
            plain = jnp.where(
                even,
                pltpu.roll(get_y(1, 0), 2 * cz - 1, 0),
                pltpu.roll(get_y(-1, 0), 1, 0),
            )
            out = [plain]
            if "z" in kinds:
                out.append(jnp.where(sub_y < 2 * last, pltpu.roll(plain, 2 * cz - 2, 0), zero))
                out.append(jnp.where(sub_y >= 2, pltpu.roll(plain, 2, 0), zero))
            if "x" in kinds:
                ahead, behind = turn(plain)
                out.append(jnp.where(lane_y < LANES - 1, ahead, zero))
                out.append(jnp.where(lane_y > 0, behind, zero))
            return out

        def pack_sides(get):
            get_y = get[2]
            pack[2 * cz : 4 * cz, :] = jnp.where(even, get_y(-1, -1), get_y(1, -1))
            pack[4 * cz : 6 * cz, :] = jnp.where(even, get_y(-1, 1), get_y(1, 1))

        def near_z(get, sz, kinds, turned):
            get_z, get_x, get_y = get
            plain = get_z(sz)
            out = [plain]
            row = last if sz == -1 else 0
            if "x" in kinds:
                zpad[8:top, :] = plain
                zpad[7:8, :] = get_x(-1, sz, 0)[row : row + 1]
                zpad[top : top + 1, :] = get_x(1, sz, 0)[row : row + 1]
                out.append(zpad[9 : top + 1, :])
                out.append(zpad[7 : top - 1, :])
            if "y" in kinds:
                first = 4 * cz - 2 if sz == -1 else 4 * cz
                side = pltpu.roll(turned, LANES - 1 - first, 1)
                out.append(pltpu.roll(jnp.where(lane == 0, side, plain), LANES - 1, 1))
                out.append(pltpu.roll(jnp.where(lane == LANES - 1, side, plain), 1, 1))
            return out

        def harmonic(own, near):
            return 2.0 * own * near / (own + near)

        ends = jnp.logical_or(lane == 0, lane == LANES - 1)

        def spread(dest, add, turned, of_x, of_z):
            for z in range(cz):
                got = jnp.where(ends, pltpu.roll(turned, LANES - 1 - 2 * z, 1), zero)
                if z == 0:
                    got = got + of_z(-1)
                if z == last:
                    got = got + of_z(1)
                if add:
                    dest[z] += got
                else:
                    dest[z] = got
            for sx, row in ((-1, 0), (1, cx - 1)):
                dest[:, row, :] += of_x(sx)

        for load in loads[:3]:
            load.wait()

        pack_faces(
            0, 0,
            lambda z: (ids_ref[z] + 1).astype(jnp.float32),
            lambda x: (ids_ref[:, x, :] + 1).astype(jnp.float32),
        )
        pack_faces(0, 1, lambda z: lp_ref[z], lambda x: lp_ref[:, x, :])
        pack_faces(0, 2, lambda z: p_ref[z], lambda x: p_ref[:, x, :])

        for c in range(classes):
            cols = [jnp.full((8, LANES), dia_ref[k, c], jnp.float32) for k in range(3)]
            for k in range(3):
                tab[k, c] = cols[k]
            for k, (a, b) in enumerate(((0, 1), (0, 2), (1, 2))):
                tab[3 + k, c] = she_ref[k, c] * jnp.sqrt(cols[a] * cols[b])
            tab[6, c] = jnp.full((8, LANES), sto_ref[c], jnp.float32)

        pack[...] = jnp.zeros_like(pack)
        for ref in (va, vap, vam, vb, vbp, vbm):
            for z in (0, cz + 1):
                ref[z] = jnp.zeros_like(ref[z])
            for lo in (0, top):
                ref[:, lo : lo + 8, :] = jnp.zeros((cz + 2, 8, LANES), jnp.float32)

        def rows_of(t):
            return pl.ds(pl.multiple_of(t * 8, 8), 8)

        def lookup(code, comps):
            found = [jnp.zeros(code.shape, jnp.float32) for _ in comps]
            for c in range(classes):
                hit = code == jnp.float32(c + 1)
                found = [
                    jnp.where(hit, jnp.broadcast_to(tab[k, c, 0:1, :], code.shape), f)
                    for k, f in zip(comps, found)
                ]
            return found

        def tensor_tile(t, carry):
            r = rows_of(t)
            out = rows_of(t + 1)
            code = (ids_ref[:, r, :] + 1).astype(jnp.float32)
            gain = jnp.exp(lp_ref[:, r, :])
            found = lookup(code, range(7))
            for k in range(6):
                value = found[k] * gain
                ten[k, 1 : cz + 1, out, :] = value
                if k in (2, 4, 5):
                    slot = (2, 4, 5).index(k)
                    ahead, behind = turn(value)
                    ten_p[slot, 1 : cz + 1, out, :] = ahead
                    ten_m[slot, 1 : cz + 1, out, :] = behind
            diag[:, r, :] = found[6]
            value = p_ref[:, r, :]
            ahead, behind = turn(value)
            va[1 : cz + 1, out, :] = value
            vap[1 : cz + 1, out, :] = ahead
            vam[1 : cz + 1, out, :] = behind
            return carry

        lax.fori_loop(0, tiles, tensor_tile, 0, unroll=2)

        pl.semaphore_wait(barrier, expected)
        start(0, X_FIRST + YZ_DIRS)

        def near_of(refs, t):
            plain, plus, minus = refs
            by_y = {0: plain, 1: plus, -1: minus}
            cache = {}

            def near(vector):
                dz, dx, dy = vector
                if (dx, dy) not in cache:
                    ref = by_y[dy]
                    r = pl.ds(t * 8 + 8 + dx, 8) if dx else rows_of(t + 1)
                    if dx and dy:
                        cache[(dx, dy)] = ref[1 : cz + 1, r, :]
                    else:
                        cache[(dx, dy)] = ref[:, r, :]
                got = cache[(dx, dy)]
                if dx and dy:
                    return got
                return got[1 + dz : 1 + dz + cz]

            return near

        zi = lax.broadcasted_iota(jnp.int32, (cz, 8, LANES), 0)
        xi = lax.broadcasted_iota(jnp.int32, (cz, 8, LANES), 1)
        yi = lax.broadcasted_iota(jnp.int32, (cz, 8, LANES), 2)

        def coef_tile(t, carry):
            r = rows_of(t)
            mid = rows_of(t + 1)
            at = (zi, xi + t * 8, yi)
            total = diag[:, r, :]
            nears = {
                0: near_of((ten.at[0], None, None), t),
                1: near_of((ten.at[1], None, None), t),
                2: near_of((ten.at[2], ten_p.at[0], ten_m.at[0]), t),
                3: near_of((ten.at[3], None, None), t),
                4: near_of((ten.at[4], ten_p.at[1], ten_m.at[1]), t),
                5: near_of((ten.at[5], ten_p.at[2], ten_m.at[2]), t),
            }
            for e, (vector, comp, sign) in enumerate(OFFSETS):
                own = ten[comp, 1 : cz + 1, mid, :]
                near = nears[comp](vector)
                if comp < 3:
                    value = harmonic(own, near)
                else:
                    value = 0.125 * sign * (own + near)
                out = None
                for axis in range(3):
                    if vector[axis] == 0:
                        continue
                    edge = shape[axis] - 1 if vector[axis] == 1 else 0
                    hit = at[axis] == edge
                    out = hit if out is None else jnp.logical_or(out, hit)
                value = jnp.where(out, zero, value)
                coef[e, :, r, :] = value
                total = total + jnp.abs(value)
            diag[:, r, :] = total
            return carry

        lax.fori_loop(0, tiles, coef_tile, 0)

        def gather(refs, t, acc):
            near = near_of(refs, t)
            r = rows_of(t)
            for e, (vector, comp, sign) in enumerate(OFFSETS):
                acc = acc + coef[e, :, r, :] * near(vector)
            return acc

        a_refs = (va, vap, vam)
        b_refs = (vb, vbp, vbm)

        loads[3].wait()

        def inside_tile(t, carry):
            r = rows_of(t)
            part[:, r, :] = gather(a_refs, t, src_ref[:, r, :])
            return carry

        lax.fori_loop(0, tiles, inside_tile, 0, unroll=4)

        arrive(0)

        gid = getters(0, 0)
        glp = getters(0, 1)

        def tensor_get(k):
            def of(which):
                def get(*args):
                    code = gid[which](*args)
                    return lookup(code, [k])[0] * jnp.exp(glp[which](*args))
                return get
            return of(0), of(1), of(2)

        gets = {k: tensor_get(k) for k in range(6)}
        rim_x = {}
        for side, sx in ((0, -1), (1, 1)):
            row = 8 if sx == -1 else top - 1
            own = {k: ten[k, 1 : cz + 1, row, :] for k in (1, 3, 5)}
            values = [harmonic(own[1], near_x(gets[1], sx, "")[0])]
            near = near_x(gets[3], sx, "z")
            for dz, got, ok in ((1, near[1], sub_x < last), (-1, near[2], sub_x > 0)):
                values.append(jnp.where(ok, 0.125 * (dz * sx) * (own[3] + got), zero))
            near = near_x(gets[5], sx, "y")
            for dy, got in ((1, near[1]), (-1, near[2])):
                values.append(0.125 * (sx * dy) * (own[5] + got))
            size = None
            for j, value in enumerate(values):
                rcx[side, j] = value
                size = jnp.abs(value) if size is None else size + jnp.abs(value)
            rim_x[sx] = size

        code = ys1[0]
        gain = jnp.exp(ys1[1])
        own = {k: f * gain for k, f in zip((2, 4, 5), lookup(code, (2, 4, 5)))}
        sy = jnp.where(even, jnp.float32(0.125), jnp.float32(-0.125))
        values = [harmonic(own[2], near_y(gets[2], "")[0])]
        near = near_y(gets[4], "z")
        for dz, got, ok in ((1, near[1], sub_y < 2 * last), (-1, near[2], sub_y >= 2)):
            values.append(jnp.where(ok, dz * sy * (own[4] + got), zero))
        near = near_y(gets[5], "x")
        for dx, got, ok in ((1, near[1], lane_y < LANES - 1), (-1, near[2], lane_y > 0)):
            values.append(jnp.where(ok, dx * sy * (own[5] + got), zero))
        size = None
        for j, value in enumerate(values):
            rcy[j] = value
            size = jnp.abs(value) if size is None else size + jnp.abs(value)
        pack[0 : 2 * cz, :] = size
        pack_sides(gets[4])
        turned = pack[...].T
        rim_z = {}
        for side, sz in ((0, -1), (1, 1)):
            z = 1 if sz == -1 else cz
            own = {k: ten[k, z, 8:top, :] for k in (0, 3, 4)}
            values = [harmonic(own[0], near_z(gets[0], sz, "", None)[0])]
            near = near_z(gets[3], sz, "x", None)
            for dx, got in ((1, near[1]), (-1, near[2])):
                values.append(0.125 * (sz * dx) * (own[3] + got))
            near = near_z(gets[4], sz, "y", turned)
            for dy, got in ((1, near[1]), (-1, near[2])):
                values.append(0.125 * (sz * dy) * (own[4] + got))
            size = None
            for j, value in enumerate(values):
                rcz[side, j] = value
                size = jnp.abs(value) if size is None else size + jnp.abs(value)
            rim_z[sz] = size
        spread(robin, False, turned, lambda sx: rim_x[sx], lambda sz: rim_z[sz])

        def scale_tile(t, carry):
            r = rows_of(t)
            rim = robin[:, r, :]
            total = diag[:, r, :] + rim
            rim = ROBIN * rim
            diag[:, r, :] = total
            robin[:, r, :] = rim
            inv[:, r, :] = 1.0 / (total + rim)
            return carry

        lax.fori_loop(0, tiles, scale_tile, 0, unroll=4)

        def weigh(weights, values):
            out = None
            for j, value in enumerate(values):
                term = weights(j) * value
                out = term if out is None else out + term
            return out

        def spread_pressure(dest, add, stage, q):
            get = getters(stage, q)
            pack[0 : 2 * cz, :] = weigh(lambda j: rcy[j], near_y(get, "zx"))
            pack_sides(get)
            turned = pack[...].T
            spread(
                dest, add, turned,
                lambda sx: weigh(lambda j: rcx[(sx + 1) // 2, j], near_x(get, sx, "zy")),
                lambda sz: weigh(lambda j: rcz[(sz + 1) // 2, j], near_z(get, sz, "xy", turned)),
            )

        def first_tile(t, carry):
            r = rows_of(t)
            mid = rows_of(t + 1)
            fixed = base[:, r, :] + robin[:, r, :] * va[1 : cz + 1, mid, :]
            u = (fixed + part[:, r, :]) * inv[:, r, :]
            base[:, r, :] = fixed + src_ref[:, r, :]
            ahead, behind = turn(u)
            vb[1 : cz + 1, mid, :] = u
            vbp[1 : cz + 1, mid, :] = ahead
            vbm[1 : cz + 1, mid, :] = behind
            return carry

        def second_tile(t, carry):
            r = rows_of(t)
            mid = rows_of(t + 1)
            u = gather(b_refs, t, base[:, r, :]) * inv[:, r, :]
            ahead, behind = turn(u)
            va[1 : cz + 1, mid, :] = u
            vap[1 : cz + 1, mid, :] = ahead
            vam[1 : cz + 1, mid, :] = behind
            return carry

        def residual_tile(t, carry):
            r = rows_of(t)
            value = va[1 : cz + 1, rows_of(t + 1), :]
            applied = src_ref[:, r, :] - diag[:, r, :] * value
            res_ref[:, r, :] = gather(a_refs, t, applied)
            return carry

        for step in range(ITERS):
            spread_pressure(base, False, step, 2 if step == 0 else 0)
            lax.fori_loop(0, tiles, first_tile, 0, unroll=4)
            lax.fori_loop(0, 2, lambda i, c: second_tile(i * (tiles - 1), c), 0, unroll=2)
            for side, x in ((0, 8), (1, top - 1)):
                stages[step + 1][1][side, 0] = va[1 : cz + 1, x, :]
            start(step + 1, X_FIRST)
            lax.fori_loop(1, tiles - 1, second_tile, 0, unroll=2)
            pack_faces(step + 1, 0, lambda z: va[z + 1, 8:top, :], None)
            start(step + 1, YZ_DIRS)
            if step == ITERS - 1:
                put_out = pltpu.make_async_copy(
                    va.at[1 : cz + 1, 8:top, :], out_hbm, load_sem.at[4]
                )
                put_out.start()
            if step == ITERS - 1:
                lax.fori_loop(0, tiles, residual_tile, 0, unroll=4)
            else:
                lax.fori_loop(0, tiles, inside_tile, 0, unroll=4)
            arrive(step + 1)
        spread_pressure(res_ref, True, ITERS, 0)
        put_res = pltpu.make_async_copy(res_ref, res_hbm, load_sem.at[5])
        put_res.start()
        put_out.wait()
        put_res.wait()

        for stage in range(ITERS + 1):
            for d in DIRS:
                @pl.when(there[d])
                def _(d=d, stage=stage):
                    copy_of(stage, d).wait_send()

    return kernel


def solution(mesh):
    sizes = tuple(mesh.shape[a] for a in AXES)

    def per_device(rock_ids, log_perm, rock_diagonal, rock_shear, rock_storage, source, pressure_start):
        shape = rock_ids.shape
        cz, cx, cy = shape
        classes = rock_storage.shape[0]
        f32 = jnp.float32
        padded = (cz + 2, cx + 16, cy)

        def exchange(nq):
            return [
                pltpu.VMEM((2, nq, cx, cy), f32),
                pltpu.VMEM((2, nq, cz, cy), f32),
                pltpu.VMEM((nq, 2 * cz, cx), f32),
                pltpu.VMEM((len(Z_DIRS), nq, cx, cy), f32),
                pltpu.VMEM((len(X_DIRS), nq, cz, cy), f32),
                pltpu.VMEM((len(Y_DIRS), nq, 2 * cz, cx), f32),
            ]

        hbm = pl.BlockSpec(memory_space=pltpu.HBM)
        smem = pl.BlockSpec(memory_space=pltpu.SMEM)
        return pl.pallas_call(
            make_kernel(sizes, shape, classes),
            out_shape=(jax.ShapeDtypeStruct(shape, f32), jax.ShapeDtypeStruct(shape, f32)),
            in_specs=[hbm, hbm, smem, smem, smem, hbm, hbm],
            out_specs=(hbm, hbm),
            scratch_shapes=[
                pltpu.VMEM((7, classes, 8, cy), f32),
                pltpu.VMEM((6,) + padded, f32),
                pltpu.VMEM((3,) + padded, f32),
                pltpu.VMEM((3,) + padded, f32),
            ]
            + [pltpu.VMEM(padded, f32)] * 6
            + [pltpu.VMEM((len(OFFSETS),) + shape, f32)]
            + [pltpu.VMEM(shape, f32)] * 5
            + [
                pltpu.VMEM((cx, cy), f32),
                pltpu.VMEM((cx + 16, cy), f32),
                pltpu.VMEM((2, 5, cz, cy), f32),
                pltpu.VMEM((5, 2 * cz, cx), f32),
                pltpu.VMEM((2, 5, cx, cy), f32),
            ]
            + exchange(3)
            + exchange(1)
            + exchange(1)
            + [pltpu.VMEM(shape, jnp.int32)]
            + [pltpu.VMEM(shape, f32)] * 4
            + [
                pltpu.SemaphoreType.DMA((6,)),
                pltpu.SemaphoreType.DMA((ITERS + 1, len(DIRS))),
                pltpu.SemaphoreType.DMA((ITERS + 1, len(DIRS))),
            ],
            compiler_params=pltpu.CompilerParams(
                collective_id=0, has_side_effects=True, vmem_limit_bytes=61440 * 1024
            ),
            name="schwarz",
        )(rock_ids, log_perm, rock_diagonal.T, rock_shear.T, rock_storage, source, pressure_start)

    block = P("gz", "gx", "gy")
    return jax.shard_map(
        per_device,
        mesh=mesh,
        in_specs=(block, block, P(), P(), P(), block, block),
        out_specs=(block, block),
        check_vma=False,
    )
```
